256 devices in a mesh: group: 8 (over x, core), dev: 32 (over y, z).
Axes of the slice: x: 4, y: 4, z: 8, core: 2. Of those that a mesh axis runs over, the one named last changes fastest.
Arguments:
- elem_ops: bfloat16 [16384, 48, 64], P(('group', 'dev')), may hold values from -0.75 to 0.75
- elem_stiff: bfloat16 [16384, 48], P(('group', 'dev')), may hold values from 0.5 to 4
- owner: int32 [16384, 1], P(('group', 'dev')), may hold values from 0 to 31; in each aligned block of 64 rows (0 to 63, 64 to 127, ...) at most 4 rows name the same one
- row_slot: int32 [16384], P(('group', 'dev')), may hold values from 0 to 63
- couplings: float32 [16384, 4, 64, 64], P(('group', 'dev')), may hold values from -0.12 to 0.12
- coupling_cols: int32 [16384, 4], P(('group', 'dev')), may hold values from 0 to 191, as said below
- mass: float32 [16384, 64], P(('group', 'dev')), may hold values from 2 to 4
- rhs: float32 [16384, 64], P(('group', 'dev')), may hold values from -48 to 48
Outputs:
- solution: float32 [16384, 64], P(('group', 'dev'))
- residual: float32 [16384, 64], P(('group', 'dev'))
The draws below stay inside these ranges and needn't reach their ends.
Inputs may be any that keep to these rules, and one draw needn't show every extreme that they name: Among the 64 elements of one device (each aligned block of 64 entries) no owner is named more than 4 times, a bound that some block reaches. `coupling_cols`: A value below 64 names a block row of the lower lateral group, one below 128 the device's own, the rest the upper lateral group, as in the operator's step.
All inputs are finite; a program needn't handle non-finite values.
Results may differ from the reference program's by a relative error of at most 0.0005.
Values may be sent and summed in bfloat16 or wider, within the bound.
No kernel may reach another device: no remote copies, remote signals or barrier semaphores. Data moves between devices by JAX's collectives and lax.ppermute only.
A program may use at most 64 MiB of HBM per device.

```python
import math
import jax
import jax.numpy as jnp
import numpy as np
from jax import lax

BS = 64
Q = 48
K = 4
ITERS = 3
R = 64
E_DEV = 64
CAP = 4
ELEMS = 16384
ROWS = 16384
N_GROUP = 8
N_DEV = 32


def draw_coupling_cols(key, part):
    region_draw = jax.random.randint(jax.random.fold_in(key, 11), (ROWS, K), 0, 4)
    region = (region_draw + 1) // 2
    within = jax.random.randint(jax.random.fold_in(key, 12), (ROWS, K), 0, R)
    return (region * R + within).astype(jnp.int32)


def place_ends(entries, rng, low, high):
    longest = entries.shape.index(max(entries.shape))
    spots = []
    for shift in (0, 1):
        where = [jax.random.randint(jax.random.fold_in(rng, axis), (), 0, length) for axis, length in enumerate(entries.shape)]
        where[longest] = (where[longest] + shift) % entries.shape[longest]
        spots.append(tuple(where))
    return entries.at[spots[0]].set(low).at[spots[1]].set(high)


def block_levels(key, shape, cuts, low, high):
    gain = 1.0
    for position, blocks in cuts:
        heights = jax.random.uniform(jax.random.fold_in(jax.random.fold_in(key, 6), position), (blocks,), jnp.float32, low / len(cuts), high / len(cuts))
        gain = gain * jnp.repeat(jnp.exp(heights), shape[position] // blocks).reshape((-1,) + (1,) * (len(shape) - 1 - position))
    return gain


def routed_block(stream_key, own, number, rows, amount, top, reach, slope):
    ranking = jax.random.permutation(stream_key, amount)
    heavy_load, ordinary = shares(amount, rows * top, reach, slope, True), shares(amount, rows * top, reach, slope, False)
    places = jnp.arange(amount)

    def named(tallies, offset_by):
        used = int((tallies > 0).sum())
        fixed = max(1, used // 4)
        shifted = fixed + (places - fixed + offset_by * (used - fixed)) % max(1, amount - fixed)
        return jnp.zeros((amount,), jnp.int32).at[ranking[jnp.where(places < fixed, places, shifted)]].set(jnp.asarray(tallies, jnp.int32))

    tallies = jnp.where(number % 4 == 0, named(heavy_load, number // 4), named(ordinary, number - number // 4 - 1))
    mixed = jax.random.permutation(jax.random.fold_in(own, 3), amount)
    source_of, taker = mixed[0:amount // 2 * 2:2], mixed[1:amount // 2 * 2:2]
    margin = jnp.minimum(tallies[source_of] - 1, reach - tallies[taker]) // 2
    margin = jnp.where((source_of == ranking[0]) | (taker == ranking[0]) | (tallies[taker] == 0), 0, jnp.maximum(margin, 0))
    shifted = jax.random.randint(jax.random.fold_in(own, 4), (amount // 2,), 0, 1 << 20) % (margin + 1)
    tallies = tallies.at[source_of].add(-shifted).at[taker].add(shifted)
    items = jnp.searchsorted(jnp.cumsum(tallies), jnp.arange(rows * top), side="right").astype(jnp.int32)
    table = items.reshape(top, rows).T
    table = table[jax.random.permutation(jax.random.fold_in(own, 1), rows)]
    offset_by = jax.random.randint(jax.random.fold_in(own, 2), (rows, 1), 0, top)
    return jnp.take_along_axis(table, (jnp.arange(top)[None, :] + offset_by) % top, axis=1)


def shares(amount, total, bound, slope, full):
    weights = [(1 << 20) // math.isqrt(standing ** slope) + 1 for standing in range(1, amount + 1)]
    largest = bound if full else min(bound, max(-(-total // amount), total * weights[0] // sum(weights)))
    least = 1 if total - largest >= amount - 1 else 0
    counts, rest = [largest] + [least] * (amount - 1), total - largest - least * (amount - 1)
    while rest > 0:
        free = [i for i in range(1, amount) if counts[i] < largest] or [i for i in range(1, amount) if counts[i] < bound]
        pool, left = sum([weights[i] for i in free]), rest
        for i in free:
            extra = min(bound - counts[i], max(1, left * weights[i] // pool), rest)
            counts[i] = counts[i] + extra
            rest = rest - extra
    return np.array(counts)


def scatter_about(own_key, shape, scale, most, shards=(), kind=jnp.bfloat16):
    entries = jax.random.normal(own_key, shape, jnp.float32) * scale
    if len(shards) > 0:
        entries = block_levels(own_key, shape, shards, -0.22, 0.18) * entries
    return jnp.clip(entries, min=-most, max=most).astype(kind)


def setup_inputs(seed: int = 0) -> dict:
    key_of = jax.random.split(jax.random.key(seed), 9)
    elem_ops = scatter_about(key_of[0], (ELEMS, Q, BS), 0.125, 0.75, ((0, 256),))
    elem_stiff = jnp.clip(jnp.exp(math.log(4.0) - 2.0794415 * jax.random.uniform(key_of[1], (ELEMS, Q), jnp.float32) ** block_levels(key_of[1], (ELEMS, Q), ((0, 256),), -0.2, 0.2)), 0.5, 4.0).astype(jnp.bfloat16)
    owner_keys = jax.random.split(jax.random.fold_in(key_of[2], 1), ELEMS // E_DEV)
    owner_turns = jax.random.permutation(jax.random.fold_in(key_of[2], 3), ELEMS // E_DEV)
    owner = jax.vmap(lambda own, number: routed_block(jax.random.fold_in(key_of[2], 2), own, number, E_DEV, N_DEV, 1, CAP, 1))(owner_keys, owner_turns).reshape((ELEMS, 1))
    row_slot = place_ends(jax.random.randint(key_of[3], (ELEMS,), 0, R), jax.random.fold_in(key_of[3], 1), 0, R - 1).astype(jnp.int32)
    couplings = scatter_about(key_of[4], (ROWS, K, BS, BS), 0.02, 0.12, ((0, 256),), jnp.float32)
    coupling_cols = draw_coupling_cols(jax.random.fold_in(key_of[8], 71), 0)
    mass = jnp.clip(jnp.exp(math.log(4.0) - 0.6931472 * jax.random.uniform(key_of[6], (ROWS, BS), jnp.float32) ** block_levels(key_of[6], (ROWS, BS), ((0, 256),), -0.2, 0.2)), 2.0, 4.0)
    rhs = scatter_about(key_of[7], (ROWS, BS), 8.0, 48.0, ((0, 256),), jnp.float32)
    return dict(elem_ops=elem_ops, elem_stiff=elem_stiff, owner=owner, row_slot=row_slot, couplings=couplings, coupling_cols=coupling_cols, mass=mass, rhs=rhs)


def element_tangents(element_ops, element_stiff):
    values = element_ops.astype(jnp.float32)
    weights = element_stiff.astype(jnp.float32)
    return jnp.einsum("eqi,eq,eqj->eij", values, weights, values, precision=lax.Precision.HIGHEST)


def reference(elem_ops, elem_stiff, owner, row_slot, couplings, coupling_cols, mass, rhs):
    blocks = ELEMS // E_DEV
    groups_of = (jnp.arange(blocks, dtype=jnp.int32) // N_DEV).astype(jnp.int32)
    inputs = (elem_ops.reshape(blocks, E_DEV, Q, BS), elem_stiff.reshape(blocks, E_DEV, Q),
              owner.reshape(blocks, E_DEV), row_slot.reshape(blocks, E_DEV), groups_of)

    def add_block(total, pieces):
        block_ops, block_stiff, block_owner, block_slot, group_here = pieces
        target = group_here * (N_DEV * R) + block_owner * R + block_slot
        return total.at[target].add(element_tangents(block_ops, block_stiff)), None

    diag_block, _ = lax.scan(add_block, jnp.zeros((ROWS, BS, BS), jnp.float32), inputs)
    cols_all = coupling_cols.reshape(N_GROUP, N_DEV, R * K)
    row_ids = jnp.arange(ROWS, dtype=jnp.int32)
    group_ids = (row_ids // (N_DEV * R)).astype(jnp.int32)
    dev_ids = ((row_ids // R) % N_DEV).astype(jnp.int32)
    region = (coupling_cols // R).astype(jnp.int32)
    target_group = (group_ids[:, None] + region - 1).astype(jnp.int32)
    valid = (target_group >= 0) & (target_group < N_GROUP)
    target_row = ((target_group * N_DEV + dev_ids[:, None]) * R + coupling_cols % R).astype(jnp.int32)
    target_row = jnp.where(valid, target_row, ROWS).astype(jnp.int32).reshape(-1)

    def apply_operator(field):
        field4 = field.reshape(N_GROUP, N_DEV, R, BS)
        zero = jnp.zeros((1, N_DEV, R, BS), jnp.float32)
        lower = jnp.concatenate([zero, field4[:-1]], axis=0)
        upper = jnp.concatenate([field4[1:], zero], axis=0)
        extended = jnp.stack([lower, field4, upper], axis=2).reshape(N_GROUP, N_DEV, 3 * R, BS)
        nearby = jnp.take_along_axis(extended, cols_all[..., None], axis=2).reshape(ROWS, K, BS)
        own_part = jnp.einsum("rij,rj->ri", diag_block, field, precision=lax.Precision.HIGHEST)
        cross = jnp.einsum("rkij,rkj->ri", couplings, nearby, precision=lax.Precision.HIGHEST)
        returned = jnp.einsum("rkij,ri->rkj", couplings, field, precision=lax.Precision.HIGHEST)
        back = jnp.zeros((ROWS + 1, BS), jnp.float32).at[target_row].add(returned.reshape(ROWS * K, BS))[:ROWS]
        return own_part + mass * field + cross + back

    solution = jnp.zeros_like(rhs)
    residual = rhs
    direction = rhs
    norm_now = jnp.sum(residual * residual)
    for iteration in range(ITERS):
        image = apply_operator(direction)
        alpha = norm_now / jnp.sum(direction * image)
        solution = solution + alpha * direction
        residual = residual - alpha * image
        norm_next = jnp.sum(residual * residual)
        direction = residual + (norm_next / norm_now) * direction
        norm_now = norm_next
    return solution, residual
```

```python
import jax
import jax.numpy as jnp
from jax import lax
from jax.sharding import PartitionSpec as P

BS = 64
K = 4
LANES = 128
ITERS = 3
SHIFT = 4.0
SCALE = 0.125
EVERY = ("group", "dev")


def shifted(shard, axis, by):
    count = lax.axis_size(axis)
    pairs = [(i, i + by) for i in range(count) if 0 <= i + by < count]
    return lax.ppermute(shard, axis, pairs)


def whole_sums(*pairs):
    parts = jnp.stack([jnp.sum(a * b) for a, b in pairs])
    members = lax.axis_size("group") * lax.axis_size("dev")
    row = jnp.pad(parts, (0, LANES - parts.shape[0]))
    got = lax.all_to_all(
        jnp.broadcast_to(row[None, :], (members, LANES)), EVERY, 0, 0, tiled=True
    )
    total = jnp.sum(got, axis=0)
    return [total[i] for i in range(len(pairs))]


def square(coefs):
    out = [0.0] * (2 * len(coefs) - 1)
    for i, a in enumerate(coefs):
        for j, b in enumerate(coefs):
            out[i + j] = out[i + j] + a * b
    return out


def plus(a, b):
    size = max(len(a), len(b))
    a, b = (list(v) + [0.0] * (size - len(v)) for v in (a, b))
    return [u + v for u, v in zip(a, b)]


def times(scalar, coefs):
    return [scalar * v for v in coefs]


def conjugate_coefficients(moments):
    x, r, p = [0.0], [1.0], [1.0]
    rr = moments[0]
    for step in range(ITERS):
        sq = square(p)
        bottom = sum(
            u * (moments[n + 1] * (1.0 / SCALE) + SHIFT * moments[n]) for n, u in enumerate(sq)
        )
        alpha = rr / bottom
        x = plus(x, times(alpha, p))
        image = plus([0.0] + times(1.0 / SCALE, p), times(SHIFT, p))
        r = plus(r, times(-alpha, image))
        if step < ITERS - 1:
            new = sum(u * moments[n] for n, u in enumerate(square(r)))
            p = plus(r, times(new / rr, p))
            rr = new
    return x, r


def combine(coefs, basis):
    total = coefs[0] * basis[0]
    for a, v in zip(coefs[1:], basis[1:]):
        total = total + a * v
    return total


def per_device(elem_ops, elem_stiff, owner, row_slot, couplings, coupling_cols, mass, rhs):
    rows_here = rhs.shape[0]
    owners = lax.axis_size("dev")
    count, strains, _ = elem_ops.shape
    capacity = 2 * count // owners
    slots = owners * capacity
    target = owner[:, 0]
    member = (target[:, None] == jnp.arange(owners, dtype=jnp.int32)[None, :]).astype(jnp.int32)
    before = jnp.cumsum(member, axis=0) - member
    position = target * capacity + jnp.sum(before * member, axis=1)
    width = strains * BS + LANES
    record = jnp.concatenate(
        [
            elem_ops.reshape(count, strains * BS),
            elem_stiff,
            row_slot.astype(jnp.bfloat16)[:, None],
            jnp.zeros((count, LANES - strains - 1), jnp.bfloat16),
        ],
        axis=1,
    )
    picker = (jnp.arange(slots, dtype=jnp.int32)[:, None] == position[None, :]).astype(jnp.bfloat16)
    packed = jnp.dot(picker, record, preferred_element_type=jnp.float32).astype(jnp.bfloat16)
    got = lax.all_to_all(
        packed.reshape(owners, capacity, width), "dev", split_axis=0, concat_axis=0, tiled=True
    ).reshape(slots, width)
    got_ops = got[:, : strains * BS].reshape(slots, strains, BS).astype(jnp.float32)
    got_stiff = got[:, strains * BS : strains * BS + strains].astype(jnp.float32)
    got_rows = got[:, strains * BS + strains].astype(jnp.int32)
    tangent = jnp.einsum(
        "eqi,eq,eqj->eij", got_ops, got_stiff, got_ops, precision=lax.Precision.HIGHEST
    ).reshape(slots, BS * BS)
    selector = (got_rows[None, :] == jnp.arange(rows_here, dtype=jnp.int32)[:, None]).astype(
        jnp.float32
    )
    diag_block = jnp.dot(selector, tangent, precision=lax.Precision.HIGHEST).reshape(
        rows_here, BS, BS
    )
    flat_cols = coupling_cols.reshape(-1)
    placer = (flat_cols[None, :] == jnp.arange(3 * rows_here, dtype=jnp.int32)[:, None]).astype(
        jnp.float32
    )

    def operator(field):
        lower = shifted(field, "group", 1)
        upper = shifted(field, "group", -1)
        returned = jnp.einsum("rkij,ri->rkj", couplings, field, precision=lax.Precision.HIGHEST)
        spread = jnp.dot(
            placer, returned.reshape(rows_here * K, BS), precision=lax.Precision.HIGHEST
        ).reshape(3, rows_here, BS)
        from_upper = shifted(spread[0], "group", -1)
        from_lower = shifted(spread[2], "group", 1)
        extended = jnp.concatenate([lower, field, upper], axis=0)
        nearby = jnp.take(extended, flat_cols, axis=0).reshape(rows_here, K, BS)
        cross = jnp.einsum("rkij,rkj->ri", couplings, nearby, precision=lax.Precision.HIGHEST)
        own = jnp.einsum("rij,rj->ri", diag_block, field, precision=lax.Precision.HIGHEST)
        return own + mass * field + cross + spread[1] + from_upper + from_lower

    basis = [rhs]
    for _ in range(ITERS):
        basis.append((operator(basis[-1]) - SHIFT * basis[-1]) * SCALE)
    moments = whole_sums(*[(basis[n // 2], basis[n - n // 2]) for n in range(2 * ITERS)])
    x_coef, r_coef = conjugate_coefficients(moments)
    return (combine(x_coef, basis), combine(r_coef, basis))


def solution(mesh):
    placed = (
        P(EVERY, None, None),
        P(EVERY, None),
        P(EVERY, None),
        P(EVERY),
        P(EVERY, None, None, None),
        P(EVERY, None),
        P(EVERY, None),
        P(EVERY, None),
    )
    return jax.shard_map(
        per_device,
        mesh=mesh,
        in_specs=placed,
        out_specs=(P(EVERY, None), P(EVERY, None)),
        check_vma=False,
    )
```

```python
import functools

import jax
import jax.numpy as jnp
from jax import lax
from jax.experimental import pallas as pl
from jax.experimental.pallas import tpu as pltpu
from jax.sharding import PartitionSpec as P

BS = 64
K = 4
LANES = 128
GROUP = 8
ROWS = 16
PER = 4
ITERS = 3
SHIFT = 4.0
SCALE = 0.125
EVERY = ("group", "dev")


def pieces(x):
    high = x.astype(jnp.bfloat16).astype(jnp.float32)
    rest = x - high
    middle = rest.astype(jnp.bfloat16).astype(jnp.float32)
    return high, middle, rest - middle


def stacked(x, axis):
    return jnp.concatenate(pieces(x), axis=axis).astype(jnp.bfloat16)


def folded(x, width):
    total = x[:, :width]
    for n in range(1, x.shape[1] // width):
        total = total + x[:, n * width : (n + 1) * width]
    return total


def iota(shape, dim):
    return lax.broadcasted_iota(jnp.int32, shape, dim)


def onehot(mask):
    return jnp.where(mask, 1.0, 0.0).astype(jnp.bfloat16)


def dot(a, b):
    return jnp.dot(a, b, preferred_element_type=jnp.float32)


def dot_nt(a, b):
    return lax.dot_general(a, b, (((1,), (1,)), ((), ())), preferred_element_type=jnp.float32)


def whole(shape):
    return pl.BlockSpec(shape, lambda *_: (0,) * len(shape))


def widen_body(blocks_ref, out_ref):
    for r in range(GROUP):
        out_ref[r * BS : (r + 1) * BS, :] = jnp.concatenate(
            [blocks_ref[r, k] for k in range(K)], axis=1
        )


def widened(couplings):
    rows = couplings.shape[0]
    return pl.pallas_call(
        widen_body,
        grid=(rows // GROUP,),
        in_specs=[pl.BlockSpec((GROUP, K, BS, BS), lambda n: (n, 0, 0, 0))],
        out_specs=pl.BlockSpec((GROUP * BS, K * BS), lambda n: (n, 0)),
        out_shape=jax.ShapeDtypeStruct((rows * BS, K * BS), jnp.float32),
    )(couplings)


def spread_body(field_ref, wide_ref, cols_ref, down_ref, here_ref, up_ref, returned_ref):
    step = pl.program_id(0)
    for g in range(ROWS // GROUP):
        base = pl.multiple_of(step * ROWS + g * GROUP, GROUP)
        tall = jnp.transpose(field_ref[pl.ds(base, GROUP), :])
        found = []
        for r in range(GROUP):
            at = (g * GROUP + r) * BS
            found.append(
                jnp.sum(wide_ref[at : at + BS, :] * tall[:, r : r + 1], axis=0, keepdims=True)
            )
        returned_ref[pl.ds(base, GROUP), :] = jnp.concatenate(found, axis=0)

    @pl.when(step == pl.num_programs(0) - 1)
    def _():
        returned = returned_ref[...]
        tall = jnp.concatenate([returned[:, k * BS : (k + 1) * BS] for k in range(K)], axis=0)
        rows = field_ref.shape[0]
        shape = (3 * rows, tall.shape[0])
        placer = onehot(iota(shape, 0) == cols_ref[...])
        spread = folded(dot(placer, stacked(tall, 1)), BS)
        field = field_ref[...]
        down_ref[...] = jnp.concatenate([field, spread[:rows]], axis=1)
        here_ref[...] = spread[rows : 2 * rows]
        up_ref[...] = jnp.concatenate([field, spread[2 * rows :]], axis=1)


def spread_of(field, wide, cols_row):
    rows = field.shape[0]
    message = jax.ShapeDtypeStruct((rows, 2 * BS), jnp.float32)
    return pl.pallas_call(
        spread_body,
        grid=(rows // ROWS,),
        in_specs=[
            whole(field.shape),
            pl.BlockSpec((ROWS * BS, K * BS), lambda n: (n, 0)),
            whole(cols_row.shape),
        ],
        out_specs=[whole((rows, 2 * BS)), whole((rows, BS)), whole((rows, 2 * BS))],
        out_shape=[message, jax.ShapeDtypeStruct(field.shape, jnp.float32), message],
        scratch_shapes=[pltpu.VMEM((rows, K * BS), jnp.float32)],
    )(field, wide, cols_row)


def cross_body(
    ends_ref, lower_ref, field_ref, upper_ref, wide_ref, cols_ref, mass_ref, here_ref, own_ref,
    out_ref, near_ref,
):
    step = pl.program_id(0)
    rows = field_ref.shape[0]
    below, above = ends_ref[0] > 0, ends_ref[1] > 0

    @pl.when(step == 0)
    def _():
        lower = jnp.where(below, lower_ref[:, :BS], 0.0)
        upper = jnp.where(above, upper_ref[:, :BS], 0.0)
        extended = stacked(jnp.concatenate([lower, field_ref[...], upper], axis=0), 1)
        lanes = iota((rows, 3 * rows), 1)
        picker = [onehot(lanes == cols_ref[:, k : k + 1]) for k in range(K)]
        near_ref[...] = jnp.concatenate([folded(dot(p, extended), BS) for p in picker], axis=1)

    same = iota((BS, BS), 0) == iota((BS, BS), 1)
    for g in range(ROWS // GROUP):
        base = pl.multiple_of(step * ROWS + g * GROUP, GROUP)
        here = pl.ds(base, GROUP)
        near = near_ref[here, :]
        found = []
        for r in range(GROUP):
            at = (g * GROUP + r) * BS
            product = wide_ref[at : at + BS, :] * near[r : r + 1, :]
            total = jnp.sum(product, axis=1, keepdims=True)
            found.append(jnp.sum(jnp.where(same, total, 0.0), axis=0, keepdims=True))
        back = jnp.where(above, upper_ref[here, BS:], 0.0) + jnp.where(
            below, lower_ref[here, BS:], 0.0
        )
        image = (
            jnp.concatenate(found, axis=0)
            + (mass_ref[here, :] - SHIFT) * field_ref[here, :]
            + here_ref[here, :]
            + own_ref[here, :]
            + back
        )
        out_ref[here, :] = image * SCALE


def cross_of(ends, lower, field, upper, wide, cols, mass, here, own):
    rows = field.shape[0]
    return pl.pallas_call(
        cross_body,
        grid=(rows // ROWS,),
        in_specs=[
            pl.BlockSpec(memory_space=pltpu.SMEM),
            whole(lower.shape),
            whole(field.shape),
            whole(upper.shape),
            pl.BlockSpec((ROWS * BS, K * BS), lambda n: (n, 0)),
            whole(cols.shape),
            whole(mass.shape),
            whole(here.shape),
            whole(own.shape),
        ],
        out_specs=whole(field.shape),
        out_shape=jax.ShapeDtypeStruct(field.shape, jnp.float32),
        scratch_shapes=[pltpu.VMEM((rows, K * BS), jnp.float32)],
    )(ends, lower, field, upper, wide, cols, mass, here, own)


def own_body(strains, field_ref, got_ref, out_ref):
    slots = got_ref.shape[0]
    tail = got_ref[:, strains * BS :].astype(jnp.float32)
    rows = tail[:, strains : strains + 1].astype(jnp.int32)
    member = jnp.where(iota((slots, LANES), 1) == rows, 1.0, 0.0)
    field = field_ref[...]
    local = folded(dot(member[:, :BS].astype(jnp.bfloat16), stacked(field, 1)), BS)
    pair = jnp.concatenate([local] * PER, axis=1)
    width = PER * BS
    strain = jnp.zeros((slots, LANES), jnp.float32)
    for n in range(strains // PER):
        ops = got_ref[:, n * width : (n + 1) * width].astype(jnp.float32)
        sums = onehot(iota((width, LANES), 1) == iota((width, LANES), 0) // BS + n * PER)
        for piece in pieces(ops * pair):
            strain = strain + dot(piece.astype(jnp.bfloat16), sums)
    stress = [p.astype(jnp.bfloat16) for p in pieces(strain * tail)]
    force = jnp.zeros((slots, width), jnp.float32)
    for n in range(strains // PER):
        ops = got_ref[:, n * width : (n + 1) * width].astype(jnp.float32)
        copies = onehot(iota((LANES, width), 0) == iota((LANES, width), 1) // BS + n * PER)
        force = force + ops * (dot(stress[0], copies) + dot(stress[1], copies) + dot(stress[2], copies))
    placer = jnp.transpose(member)[:BS].astype(jnp.bfloat16)
    out_ref[...] = folded(dot(placer, stacked(folded(force, BS), 1)), BS)


def own_of(field, got, strains):
    return pl.pallas_call(
        functools.partial(own_body, strains),
        out_shape=jax.ShapeDtypeStruct(field.shape, jnp.float32),
    )(field, got)


def sums_body(w0_ref, w1_ref, w2_ref, w3_ref, out_ref):
    basis = [w0_ref[...], w1_ref[...], w2_ref[...], w3_ref[...]]
    lane = iota((1, LANES), 1)
    row = jnp.zeros((1, LANES), jnp.float32)
    for n in range(2 * ITERS):
        product = basis[n // 2] * basis[n - n // 2]
        total = jnp.sum(jnp.sum(product, axis=0, keepdims=True), axis=1, keepdims=True)
        row = jnp.where(lane == n, total, row)
    out_ref[...] = jnp.broadcast_to(row, out_ref.shape)


def finish_body(got_ref, w0_ref, w1_ref, w2_ref, w3_ref, solution_ref, residual_ref):
    total = jnp.sum(got_ref[...], axis=0, keepdims=True)
    moments = [total[:, n : n + 1] for n in range(2 * ITERS)]
    x_coef, r_coef = conjugate_coefficients(moments)
    basis = [w0_ref[...], w1_ref[...], w2_ref[...], w3_ref[...]]
    solution_ref[...] = combine(x_coef, basis)
    residual_ref[...] = combine(r_coef, basis)


def ring(shard, axis, by):
    count = lax.axis_size(axis)
    return lax.ppermute(shard, axis, [(i, (i + by) % count) for i in range(count)])


def square(coefs):
    out = [0.0] * (2 * len(coefs) - 1)
    for i, a in enumerate(coefs):
        for j, b in enumerate(coefs):
            out[i + j] = out[i + j] + a * b
    return out


def plus(a, b):
    size = max(len(a), len(b))
    a, b = (list(v) + [0.0] * (size - len(v)) for v in (a, b))
    return [u + v for u, v in zip(a, b)]


def times(scalar, coefs):
    return [scalar * v for v in coefs]


def conjugate_coefficients(moments):
    x, r, p = [0.0], [1.0], [1.0]
    rr = moments[0]
    for step in range(ITERS):
        sq = square(p)
        bottom = sum(
            u * (moments[n + 1] * (1.0 / SCALE) + SHIFT * moments[n]) for n, u in enumerate(sq)
        )
        alpha = rr / bottom
        x = plus(x, times(alpha, p))
        image = plus([0.0] + times(1.0 / SCALE, p), times(SHIFT, p))
        r = plus(r, times(-alpha, image))
        if step < ITERS - 1:
            new = sum(u * moments[n] for n, u in enumerate(square(r)))
            p = plus(r, times(new / rr, p))
            rr = new
    return x, r


def combine(coefs, basis):
    total = coefs[0] * basis[0]
    for a, v in zip(coefs[1:], basis[1:]):
        total = total + a * v
    return total


def per_device(elem_ops, elem_stiff, owner, row_slot, couplings, coupling_cols, mass, rhs):
    rows_here = rhs.shape[0]
    owners = lax.axis_size("dev")
    count, strains, _ = elem_ops.shape
    capacity = 2 * count // owners
    slots = owners * capacity
    target = owner[:, 0]
    member = (target[:, None] == jnp.arange(owners, dtype=jnp.int32)[None, :]).astype(jnp.int32)
    before = jnp.cumsum(member, axis=0) - member
    position = target * capacity + jnp.sum(before * member, axis=1)
    width = strains * BS + LANES
    record = jnp.concatenate(
        [
            elem_ops.reshape(count, strains * BS),
            elem_stiff,
            row_slot.astype(jnp.bfloat16)[:, None],
            jnp.zeros((count, LANES - strains - 1), jnp.bfloat16),
        ],
        axis=1,
    )
    picker = (jnp.arange(slots, dtype=jnp.int32)[:, None] == position[None, :]).astype(jnp.bfloat16)
    packed = jnp.dot(picker, record, preferred_element_type=jnp.float32).astype(jnp.bfloat16)
    got = lax.all_to_all(
        packed.reshape(owners, capacity, width), "dev", split_axis=0, concat_axis=0, tiled=True
    ).reshape(slots, width)
    cols_row = coupling_cols.T.reshape(1, K * rows_here)
    wide = widened(couplings)
    place = lax.axis_index("group")
    ends = jnp.stack([place, lax.axis_size("group") - 1 - place]).astype(jnp.int32)

    def operator(field):
        down, here, up = spread_of(field, wide, cols_row)
        lower = ring(up, "group", 1)
        upper = ring(down, "group", -1)
        own = own_of(field, got, strains)
        return cross_of(ends, lower, field, upper, wide, coupling_cols, mass, here, own)

    basis = [rhs]
    for _ in range(ITERS):
        basis.append(operator(basis[-1]))
    members = lax.axis_size("group") * lax.axis_size("dev")
    parts = pl.pallas_call(
        sums_body, out_shape=jax.ShapeDtypeStruct((members, LANES), jnp.float32)
    )(*basis)
    got_parts = lax.all_to_all(parts, EVERY, 0, 0, tiled=True)
    result = jax.ShapeDtypeStruct(rhs.shape, jnp.float32)
    return tuple(pl.pallas_call(finish_body, out_shape=[result, result])(got_parts, *basis))


def solution(mesh):
    placed = (
        P(EVERY, None, None),
        P(EVERY, None),
        P(EVERY, None),
        P(EVERY),
        P(EVERY, None, None, None),
        P(EVERY, None),
        P(EVERY, None),
        P(EVERY, None),
    )
    return jax.shard_map(
        per_device,
        mesh=mesh,
        in_specs=placed,
        out_specs=(P(EVERY, None), P(EVERY, None)),
        check_vma=False,
    )
```

```python
import functools

import jax
import jax.numpy as jnp
from jax import lax
from jax.experimental import pallas as pl
from jax.experimental.pallas import tpu as pltpu
from jax.sharding import PartitionSpec as P

BS = 64
K = 4
LANES = 128
GROUP = 8
ROWS = 16
PER = 4
ITERS = 3
SHIFT = 4.0
SCALE = 0.125
LIMIT = pltpu.CompilerParams(vmem_limit_bytes=16 * 1024 * 1024)
WORK = pl.CostEstimate(flops=2_000_000_000, transcendentals=0, bytes_accessed=4_194_304)
EVERY = ("group", "dev")


def pieces(x):
    high = x.astype(jnp.bfloat16).astype(jnp.float32)
    rest = x - high
    middle = rest.astype(jnp.bfloat16).astype(jnp.float32)
    return high, middle, rest - middle


def stacked(x, axis):
    return jnp.concatenate(pieces(x), axis=axis).astype(jnp.bfloat16)


def folded(x, width):
    total = x[:, :width]
    for n in range(1, x.shape[1] // width):
        total = total + x[:, n * width : (n + 1) * width]
    return total


def iota(shape, dim):
    return lax.broadcasted_iota(jnp.int32, shape, dim)


def onehot(mask):
    return jnp.where(mask, 1.0, 0.0).astype(jnp.bfloat16)


def dot(a, b):
    return jnp.dot(a, b, preferred_element_type=jnp.float32)


def dot_nt(a, b):
    return lax.dot_general(a, b, (((1,), (1,)), ((), ())), preferred_element_type=jnp.float32)


def whole(shape):
    return pl.BlockSpec(shape, lambda *_: (0,) * len(shape))


def widen_body(blocks_ref, out_ref):
    for r in range(GROUP):
        out_ref[r * BS : (r + 1) * BS, :] = jnp.concatenate(
            [blocks_ref[r, k] for k in range(K)], axis=1
        )


def widened(couplings):
    rows = couplings.shape[0]
    return pl.pallas_call(
        widen_body,
        grid=(rows // GROUP,),
        in_specs=[pl.BlockSpec((GROUP, K, BS, BS), lambda n: (n, 0, 0, 0))],
        out_specs=pl.BlockSpec((GROUP * BS, K * BS), lambda n: (n, 0)),
        compiler_params=LIMIT,
        cost_estimate=WORK,
        out_shape=jax.ShapeDtypeStruct((rows * BS, K * BS), jnp.float32),
    )(pltpu.with_memory_space_constraint(couplings, pltpu.HBM))


def spread_body(field_ref, wide_ref, cols_ref, down_ref, here_ref, up_ref, returned_ref):
    step = pl.program_id(0)
    for g in range(ROWS // GROUP):
        base = pl.multiple_of(step * ROWS + g * GROUP, GROUP)
        tall = jnp.transpose(field_ref[pl.ds(base, GROUP), :])
        found = []
        for r in range(GROUP):
            at = (g * GROUP + r) * BS
            found.append(
                jnp.sum(wide_ref[at : at + BS, :] * tall[:, r : r + 1], axis=0, keepdims=True)
            )
        returned_ref[pl.ds(base, GROUP), :] = jnp.concatenate(found, axis=0)

    @pl.when(step == pl.num_programs(0) - 1)
    def _():
        returned = returned_ref[...]
        tall = jnp.concatenate([returned[:, k * BS : (k + 1) * BS] for k in range(K)], axis=0)
        rows = field_ref.shape[0]
        shape = (3 * rows, tall.shape[0])
        placer = onehot(iota(shape, 0) == cols_ref[...])
        spread = folded(dot(placer, stacked(tall, 1)), BS)
        field = field_ref[...]
        down_ref[...] = jnp.concatenate([field, spread[:rows]], axis=1)
        here_ref[...] = spread[rows : 2 * rows]
        up_ref[...] = jnp.concatenate([field, spread[2 * rows :]], axis=1)


def spread_of(field, wide, cols_row):
    rows = field.shape[0]
    message = jax.ShapeDtypeStruct((rows, 2 * BS), jnp.float32)
    return pl.pallas_call(
        spread_body,
        grid=(rows // ROWS,),
        in_specs=[
            whole(field.shape),
            pl.BlockSpec((ROWS * BS, K * BS), lambda n: (n, 0)),
            whole(cols_row.shape),
        ],
        out_specs=[whole((rows, 2 * BS)), whole((rows, BS)), whole((rows, 2 * BS))],
        compiler_params=LIMIT,
        cost_estimate=WORK,
        out_shape=[message, jax.ShapeDtypeStruct(field.shape, jnp.float32), message],
        scratch_shapes=[pltpu.VMEM((rows, K * BS), jnp.float32)],
    )(field, wide, cols_row)


def cross_body(final, *refs):
    ends_ref, lower_ref, field_ref, upper_ref, wide_ref, cols_ref, mass_ref, here_ref = refs[:8]
    out_ref, near_ref = refs[-2:]
    step = pl.program_id(0)
    rows = field_ref.shape[0]
    below, above = ends_ref[0] > 0, ends_ref[1] > 0

    @pl.when(step == 0)
    def _():
        lower = jnp.where(below, lower_ref[:, :BS], 0.0)
        upper = jnp.where(above, upper_ref[:, :BS], 0.0)
        extended = stacked(jnp.concatenate([lower, field_ref[...], upper], axis=0), 1)
        lanes = iota((rows, 3 * rows), 1)
        picker = [onehot(lanes == cols_ref[:, k : k + 1]) for k in range(K)]
        near_ref[...] = jnp.concatenate([folded(dot(p, extended), BS) for p in picker], axis=1)

    same = iota((BS, BS), 0) == iota((BS, BS), 1)
    for g in range(ROWS // GROUP):
        base = pl.multiple_of(step * ROWS + g * GROUP, GROUP)
        here = pl.ds(base, GROUP)
        near = near_ref[here, :]
        found = []
        for r in range(GROUP):
            at = (g * GROUP + r) * BS
            product = wide_ref[at : at + BS, :] * near[r : r + 1, :]
            total = jnp.sum(product, axis=1, keepdims=True)
            found.append(jnp.sum(jnp.where(same, total, 0.0), axis=0, keepdims=True))
        back = jnp.where(above, upper_ref[here, BS:], 0.0) + jnp.where(
            below, lower_ref[here, BS:], 0.0
        )
        image = (
            jnp.concatenate(found, axis=0)
            + (mass_ref[here, :] - SHIFT) * field_ref[here, :]
            + here_ref[here, :]
            + back
        )
        out_ref[here, :] = (image + refs[8][here, :]) * SCALE if final else image


def cross_of(ends, lower, field, upper, wide, cols, mass, here, own=None):
    rows = field.shape[0]
    operands = (ends, lower, field, upper, wide, cols, mass, here)
    operands = operands if own is None else (*operands, own)
    return pl.pallas_call(
        functools.partial(cross_body, own is not None),
        grid=(rows // ROWS,),
        in_specs=[
            pl.BlockSpec(memory_space=pltpu.SMEM),
            whole(lower.shape),
            whole(field.shape),
            whole(upper.shape),
            pl.BlockSpec((ROWS * BS, K * BS), lambda n: (n, 0)),
            whole(cols.shape),
            whole(mass.shape),
            *[whole(field.shape)] * (len(operands) - 7),
        ],
        out_specs=whole(field.shape),
        compiler_params=LIMIT,
        cost_estimate=WORK,
        out_shape=jax.ShapeDtypeStruct(field.shape, jnp.float32),
        scratch_shapes=[pltpu.VMEM((rows, K * BS), jnp.float32)],
    )(*operands)


def pack_body(capacity, ops_ref, stiff_ref, owner_ref, slot_ref, out_ref):
    owners, _, width = out_ref.shape
    slots = owners * capacity
    strains, count = stiff_ref.shape
    owner = owner_ref[...]
    across = jnp.broadcast_to(owner.astype(jnp.float32), (count, count))
    earlier = (across == jnp.transpose(across)) & (
        iota((count, count), 0) < iota((count, count), 1)
    )
    rank = jnp.sum(jnp.where(earlier, 1.0, 0.0), axis=0, keepdims=True).astype(jnp.int32)
    picker = onehot(iota((slots, count), 0) == owner * capacity + rank)
    body = strains * BS
    for at in range(0, body, 4 * LANES):
        lanes = slice(at, at + 4 * LANES)
        out_ref[:, :, lanes] = (
            dot(picker, ops_ref[:, lanes]).reshape(owners, capacity, -1).astype(jnp.bfloat16)
        )
    tail = jnp.concatenate(
        [
            stiff_ref[...].astype(jnp.float32),
            slot_ref[...].astype(jnp.float32),
            jnp.zeros((width - body - strains - 1, count), jnp.float32),
        ],
        axis=0,
    )
    ends = dot_nt(picker, tail.astype(jnp.bfloat16))
    out_ref[:, :, body:] = ends.reshape(owners, capacity, -1).astype(jnp.bfloat16)


def pack(ops, stiff, owner, slot, slots, capacity):
    body = ops.shape[1]
    return pl.pallas_call(
        functools.partial(pack_body, capacity),
        compiler_params=LIMIT,
        cost_estimate=WORK,
        out_shape=jax.ShapeDtypeStruct((slots // capacity, capacity, body + LANES), jnp.bfloat16),
    )(ops, *(pltpu.with_memory_space_constraint(v, pltpu.HBM) for v in (stiff, owner, slot)))


def own_body(strains, final, *refs):
    field_ref, got_ref, rest_ref, out_ref = refs if final else (*refs[:2], None, refs[2])
    slots = got_ref.shape[0]
    tail = got_ref[:, strains * BS :].astype(jnp.float32)
    rows = tail[:, strains : strains + 1].astype(jnp.int32)
    member = jnp.where(iota((slots, LANES), 1) == rows, 1.0, 0.0)
    field = field_ref[...]
    local = folded(dot(member[:, :BS].astype(jnp.bfloat16), stacked(field, 1)), BS)
    pair = jnp.concatenate([local] * PER, axis=1)
    width = PER * BS
    strain = jnp.zeros((slots, LANES), jnp.float32)
    for n in range(strains // PER):
        ops = got_ref[:, n * width : (n + 1) * width].astype(jnp.float32)
        sums = onehot(iota((width, LANES), 1) == iota((width, LANES), 0) // BS + n * PER)
        for piece in pieces(ops * pair):
            strain = strain + dot(piece.astype(jnp.bfloat16), sums)
    stress = [p.astype(jnp.bfloat16) for p in pieces(strain * tail)]
    force = jnp.zeros((slots, width), jnp.float32)
    for n in range(strains // PER):
        ops = got_ref[:, n * width : (n + 1) * width].astype(jnp.float32)
        copies = onehot(iota((LANES, width), 0) == iota((LANES, width), 1) // BS + n * PER)
        force = force + ops * (dot(stress[0], copies) + dot(stress[1], copies) + dot(stress[2], copies))
    placer = jnp.transpose(member)[:BS].astype(jnp.bfloat16)
    own = folded(dot(placer, stacked(folded(force, BS), 1)), BS)
    out_ref[...] = (rest_ref[...] + own) * SCALE if final else own


def own_of(field, got, strains, rest=None):
    operands = (field, got) if rest is None else (field, got, rest)
    return pl.pallas_call(
        functools.partial(own_body, strains, rest is not None),
        compiler_params=LIMIT,
        cost_estimate=WORK,
        out_shape=jax.ShapeDtypeStruct(field.shape, jnp.float32),
    )(*operands)


def sums_body(w0_ref, w1_ref, w2_ref, w3_ref, out_ref):
    basis = [w0_ref[...], w1_ref[...], w2_ref[...], w3_ref[...]]
    lane = iota((1, LANES), 1)
    row = jnp.zeros((1, LANES), jnp.float32)
    for n in range(2 * ITERS):
        product = basis[n // 2] * basis[n - n // 2]
        total = jnp.sum(jnp.sum(product, axis=0, keepdims=True), axis=1, keepdims=True)
        row = jnp.where(lane == n, total, row)
    out_ref[...] = jnp.broadcast_to(row, out_ref.shape)


def finish_body(got_ref, w0_ref, w1_ref, w2_ref, w3_ref, solution_ref, residual_ref):
    total = jnp.sum(got_ref[...], axis=0, keepdims=True)
    moments = [total[:, n : n + 1] for n in range(2 * ITERS)]
    x_coef, r_coef = conjugate_coefficients(moments)
    basis = [w0_ref[...], w1_ref[...], w2_ref[...], w3_ref[...]]
    solution_ref[...] = combine(x_coef, basis)
    residual_ref[...] = combine(r_coef, basis)


def ring(shard, axis, by):
    count = lax.axis_size(axis)
    return lax.ppermute(shard, axis, [(i, (i + by) % count) for i in range(count)])


def square(coefs):
    out = [0.0] * (2 * len(coefs) - 1)
    for i, a in enumerate(coefs):
        for j, b in enumerate(coefs):
            out[i + j] = out[i + j] + a * b
    return out


def plus(a, b):
    size = max(len(a), len(b))
    a, b = (list(v) + [0.0] * (size - len(v)) for v in (a, b))
    return [u + v for u, v in zip(a, b)]


def times(scalar, coefs):
    return [scalar * v for v in coefs]


def conjugate_coefficients(moments):
    x, r, p = [0.0], [1.0], [1.0]
    rr = moments[0]
    for step in range(ITERS):
        sq = square(p)
        bottom = sum(
            u * (moments[n + 1] * (1.0 / SCALE) + SHIFT * moments[n]) for n, u in enumerate(sq)
        )
        alpha = rr / bottom
        x = plus(x, times(alpha, p))
        image = plus([0.0] + times(1.0 / SCALE, p), times(SHIFT, p))
        r = plus(r, times(-alpha, image))
        if step < ITERS - 1:
            new = sum(u * moments[n] for n, u in enumerate(square(r)))
            p = plus(r, times(new / rr, p))
            rr = new
    return x, r


def combine(coefs, basis):
    total = coefs[0] * basis[0]
    for a, v in zip(coefs[1:], basis[1:]):
        total = total + a * v
    return total


def per_device(elem_ops, elem_stiff, owner, row_slot, couplings, coupling_cols, mass, rhs):
    rows_here = rhs.shape[0]
    owners = lax.axis_size("dev")
    count, strains, _ = elem_ops.shape
    capacity = 2 * count // owners
    slots = owners * capacity
    packed = pack(
        elem_ops.reshape(count, strains * BS), elem_stiff.T, owner.T, row_slot[None, :], slots, capacity
    )
    got = lax.all_to_all(
        packed, "dev", split_axis=0, concat_axis=0, tiled=True
    ).reshape(slots, -1)
    cols_row = coupling_cols.T.reshape(1, K * rows_here)
    wide = widened(couplings)
    place = lax.axis_index("group")
    ends = jnp.stack([place, lax.axis_size("group") - 1 - place]).astype(jnp.int32)

    basis = [rhs]
    for power in range(ITERS):
        field = basis[-1]
        down, here, up = spread_of(field, wide, cols_row)
        lower = ring(up, "group", 1)
        upper = ring(down, "group", -1)
        known = (ends, lower, field, upper, wide, coupling_cols, mass, here)
        if power == 0:
            basis.append(own_of(field, got, strains, cross_of(*known)))
        else:
            basis.append(cross_of(*known, own_of(field, got, strains)))
    members = lax.axis_size("group") * lax.axis_size("dev")
    parts = pl.pallas_call(
        sums_body, compiler_params=LIMIT, out_shape=jax.ShapeDtypeStruct((members, LANES), jnp.float32)
    )(*basis)
    got_parts = lax.all_to_all(parts, EVERY, 0, 0, tiled=True)
    result = jax.ShapeDtypeStruct(rhs.shape, jnp.float32)
    return tuple(
        pl.pallas_call(finish_body, compiler_params=LIMIT, out_shape=[result, result])(got_parts, *basis)
    )


def solution(mesh):
    placed = (
        P(EVERY, None, None),
        P(EVERY, None),
        P(EVERY, None),
        P(EVERY),
        P(EVERY, None, None, None),
        P(EVERY, None),
        P(EVERY, None),
        P(EVERY, None),
    )
    return jax.shard_map(
        per_device,
        mesh=mesh,
        in_specs=placed,
        out_specs=(P(EVERY, None), P(EVERY, None)),
        check_vma=False,
    )
```

```python
import functools

import jax
import jax.numpy as jnp
from jax import lax
from jax.experimental import pallas as pl
from jax.experimental.pallas import tpu as pltpu
from jax.sharding import PartitionSpec as P

BS = 64
K = 4
LANES = 128
GROUP = 8
ROWS = 16
PER = 4
ITERS = 3
SHIFT = 4.0
SCALE = 0.125
LIMIT = pltpu.CompilerParams(vmem_limit_bytes=16 * 1024 * 1024)
WORK = pl.CostEstimate(flops=2_000_000_000, transcendentals=0, bytes_accessed=4_194_304)
EVERY = ("group", "dev")


def pieces(x):
    high = x.astype(jnp.bfloat16).astype(jnp.float32)
    rest = x - high
    middle = rest.astype(jnp.bfloat16).astype(jnp.float32)
    return high, middle, rest - middle


def stacked(x, axis):
    return jnp.concatenate(pieces(x), axis=axis).astype(jnp.bfloat16)


def folded(x, width):
    total = x[:, :width]
    for n in range(1, x.shape[1] // width):
        total = total + x[:, n * width : (n + 1) * width]
    return total


def iota(shape, dim):
    return lax.broadcasted_iota(jnp.int32, shape, dim)


def onehot(mask):
    return jnp.where(mask, 1.0, 0.0).astype(jnp.bfloat16)


def dot(a, b):
    return jnp.dot(a, b, preferred_element_type=jnp.float32)


def dot_nt(a, b):
    return lax.dot_general(a, b, (((1,), (1,)), ((), ())), preferred_element_type=jnp.float32)


def whole(shape):
    return pl.BlockSpec(shape, lambda *_: (0,) * len(shape))


def widen_body(blocks_ref, out_ref):
    for r in range(GROUP):
        out_ref[r * BS : (r + 1) * BS, :] = jnp.concatenate(
            [blocks_ref[r, k] for k in range(K)], axis=1
        )


def widened(couplings):
    rows = couplings.shape[0]
    return pl.pallas_call(
        widen_body,
        grid=(rows // GROUP,),
        in_specs=[pl.BlockSpec((GROUP, K, BS, BS), lambda n: (n, 0, 0, 0))],
        out_specs=pl.BlockSpec((GROUP * BS, K * BS), lambda n: (n, 0)),
        compiler_params=LIMIT,
        cost_estimate=WORK,
        out_shape=jax.ShapeDtypeStruct((rows * BS, K * BS), jnp.float32),
    )(pltpu.with_memory_space_constraint(couplings, pltpu.HBM))


def spread_rows(step, block, field_ref, wide_ref, returned_ref):
    for g in range(ROWS // GROUP):
        base = step * ROWS + g * GROUP
        base = base if isinstance(base, int) else pl.multiple_of(base, GROUP)
        tall = jnp.transpose(field_ref[pl.ds(base, GROUP), :])
        found = []
        for r in range(GROUP):
            at = (block * ROWS + g * GROUP + r) * BS
            found.append(
                jnp.sum(wide_ref[pl.ds(at, BS), :] * tall[:, r : r + 1], axis=0, keepdims=True)
            )
        returned_ref[pl.ds(base, GROUP), :] = jnp.concatenate(found, axis=0)


def spread_messages(field_ref, cols_ref, down_ref, here_ref, up_ref, returned_ref):
    returned = returned_ref[...]
    tall = jnp.concatenate([returned[:, k * BS : (k + 1) * BS] for k in range(K)], axis=0)
    rows = field_ref.shape[0]
    shape = (3 * rows, tall.shape[0])
    placer = onehot(iota(shape, 0) == cols_ref[...])
    spread = folded(dot(placer, stacked(tall, 1)), BS)
    field = field_ref[...]
    down_ref[...] = jnp.concatenate([field, spread[:rows]], axis=1)
    here_ref[...] = spread[rows : 2 * rows]
    up_ref[...] = jnp.concatenate([field, spread[2 * rows :]], axis=1)


def spread_body(field_ref, wide_ref, cols_ref, down_ref, here_ref, up_ref, returned_ref):
    step = pl.program_id(0)
    spread_rows(step, 0, field_ref, wide_ref, returned_ref)

    @pl.when(step == pl.num_programs(0) - 1)
    def _():
        spread_messages(field_ref, cols_ref, down_ref, here_ref, up_ref, returned_ref)


def spread_of(field, wide, cols_row):
    rows = field.shape[0]
    message = jax.ShapeDtypeStruct((rows, 2 * BS), jnp.float32)
    return pl.pallas_call(
        spread_body,
        grid=(rows // ROWS,),
        in_specs=[
            whole(field.shape),
            pl.BlockSpec((ROWS * BS, K * BS), lambda n: (n, 0)),
            whole(cols_row.shape),
        ],
        out_specs=[whole((rows, 2 * BS)), whole((rows, BS)), whole((rows, 2 * BS))],
        compiler_params=LIMIT,
        cost_estimate=WORK,
        out_shape=[message, jax.ShapeDtypeStruct(field.shape, jnp.float32), message],
        scratch_shapes=[pltpu.VMEM((rows, K * BS), jnp.float32)],
    )(field, wide, cols_row)


def arrived(ends_ref, lower, upper):
    return jnp.where(ends_ref[0] > 0, lower, 0.0), jnp.where(ends_ref[1] > 0, upper, 0.0)


def cross_body(extra, last, *refs):
    ends_ref, lower_ref, field_ref, upper_ref, wide_ref, cols_ref, mass_ref = refs[:7]
    added, rest = refs[7 : 7 + extra], refs[7 + extra :]
    if last:
        *earlier, out_ref, sums_ref, near_ref, twice_ref = rest
        out_refs = (out_ref, sums_ref)
    else:
        *out_refs, near_ref = rest
    step = pl.program_id(0)
    rows = field_ref.shape[0]

    @pl.when(step == 0)
    def _():
        lower, upper = arrived(ends_ref, lower_ref[:, :BS], upper_ref[:, :BS])
        extended = stacked(jnp.concatenate([lower, field_ref[...], upper], axis=0), 1)
        lanes = iota((rows, 3 * rows), 1)
        picker = [onehot(lanes == cols_ref[:, k : k + 1]) for k in range(K)]
        near_ref[...] = jnp.concatenate([folded(dot(p, extended), BS) for p in picker], axis=1)

    same = iota((BS, BS), 0) == iota((BS, BS), 1)
    for g in range(ROWS // GROUP):
        base = pl.multiple_of(step * ROWS + g * GROUP, GROUP)
        here = pl.ds(base, GROUP)
        near = near_ref[here, :]
        found = []
        for r in range(GROUP):
            at = (g * GROUP + r) * BS
            product = wide_ref[at : at + BS, :] * near[r : r + 1, :]
            total = jnp.sum(product, axis=1, keepdims=True)
            found.append(jnp.sum(jnp.where(same, total, 0.0), axis=0, keepdims=True))
        cross = jnp.concatenate(found, axis=0)
        image = cross + (mass_ref[here, :] - SHIFT) * field_ref[here, :]
        for ref in added:
            image = image + ref[here, :]
        if last:
            out_refs[0][here, :] = image
            twice_ref[here, :] = image + cross
        else:
            lower, upper = arrived(ends_ref, lower_ref[here, BS:], upper_ref[here, BS:])
            image = image + (lower + upper)
            out_refs[0][here, :] = image * SCALE if extra == 2 else image

    if last:

        @pl.when(step == pl.num_programs(0) - 1)
        def _():
            fourth = twice_ref[...] * SCALE
            basis = [ref[...] for ref in earlier] + [field_ref[...], fourth]
            lane = iota((1, LANES), 1)
            row = jnp.zeros((1, LANES), jnp.float32)
            for n in range(2 * ITERS):
                product = basis[n // 2] * basis[n - n // 2]
                total = jnp.sum(jnp.sum(product, axis=0, keepdims=True), axis=1, keepdims=True)
                row = jnp.where(lane == n, total, row)
            out_refs[1][...] = jnp.broadcast_to(row, out_refs[1].shape)


def cross_of(ends, lower, field, upper, wide, cols, mass, *added, earlier=(), members=0):
    rows = field.shape[0]
    last = len(earlier) > 0
    vector = jax.ShapeDtypeStruct(field.shape, jnp.float32)
    results = [vector] + [jax.ShapeDtypeStruct((members, LANES), jnp.float32)] * last
    found = pl.pallas_call(
        functools.partial(cross_body, len(added), last),
        grid=(rows // ROWS,),
        in_specs=[
            pl.BlockSpec(memory_space=pltpu.SMEM),
            whole(lower.shape),
            whole(field.shape),
            whole(upper.shape),
            pl.BlockSpec((ROWS * BS, K * BS), lambda n: (n, 0)),
            whole(cols.shape),
            *[whole(field.shape)] * (1 + len(added) + len(earlier)),
        ],
        out_specs=[whole(v.shape) for v in results],
        compiler_params=LIMIT,
        cost_estimate=WORK,
        out_shape=results,
        scratch_shapes=[pltpu.VMEM((rows, K * BS), jnp.float32)]
        + [pltpu.VMEM(field.shape, jnp.float32)] * last,
    )(ends, lower, field, upper, wide, cols, mass, *added, *earlier)
    return found if last else found[0]


def pack_body(capacity, ops_ref, stiff_ref, owner_ref, slot_ref, out_ref):
    owners, _, width = out_ref.shape
    slots = owners * capacity
    strains, count = stiff_ref.shape
    owner = owner_ref[...]
    across = jnp.broadcast_to(owner.astype(jnp.float32), (count, count))
    earlier = (across == jnp.transpose(across)) & (
        iota((count, count), 0) < iota((count, count), 1)
    )
    rank = jnp.sum(jnp.where(earlier, 1.0, 0.0), axis=0, keepdims=True).astype(jnp.int32)
    picker = onehot(iota((slots, count), 0) == owner * capacity + rank)
    body = strains * BS
    for at in range(0, body, 4 * LANES):
        lanes = slice(at, at + 4 * LANES)
        out_ref[:, :, lanes] = (
            dot(picker, ops_ref[:, lanes]).reshape(owners, capacity, -1).astype(jnp.bfloat16)
        )
    tail = jnp.concatenate(
        [
            stiff_ref[...].astype(jnp.float32),
            slot_ref[...].astype(jnp.float32),
            jnp.zeros((width - body - strains - 1, count), jnp.float32),
        ],
        axis=0,
    )
    ends = dot_nt(picker, tail.astype(jnp.bfloat16))
    out_ref[:, :, body:] = ends.reshape(owners, capacity, -1).astype(jnp.bfloat16)


def pack(ops, stiff, owner, slot, slots, capacity):
    body = ops.shape[1]
    return pl.pallas_call(
        functools.partial(pack_body, capacity),
        compiler_params=LIMIT,
        cost_estimate=WORK,
        out_shape=jax.ShapeDtypeStruct((slots // capacity, capacity, body + LANES), jnp.bfloat16),
    )(ops, *(pltpu.with_memory_space_constraint(v, pltpu.HBM) for v in (stiff, owner, slot)))


def own_part(strains, field, got_ref):
    slots = got_ref.shape[0]
    tail = got_ref[:, strains * BS :].astype(jnp.float32)
    rows = tail[:, strains : strains + 1].astype(jnp.int32)
    member = jnp.where(iota((slots, LANES), 1) == rows, 1.0, 0.0)
    local = folded(dot(member[:, :BS].astype(jnp.bfloat16), stacked(field, 1)), BS)
    pair = jnp.concatenate([local] * PER, axis=1)
    width = PER * BS
    strain = jnp.zeros((slots, LANES), jnp.float32)
    for n in range(strains // PER):
        ops = got_ref[:, n * width : (n + 1) * width].astype(jnp.float32)
        sums = onehot(iota((width, LANES), 1) == iota((width, LANES), 0) // BS + n * PER)
        for piece in pieces(ops * pair):
            strain = strain + dot(piece.astype(jnp.bfloat16), sums)
    stress = [p.astype(jnp.bfloat16) for p in pieces(strain * tail)]
    force = jnp.zeros((slots, width), jnp.float32)
    for n in range(strains // PER):
        ops = got_ref[:, n * width : (n + 1) * width].astype(jnp.float32)
        copies = onehot(iota((LANES, width), 0) == iota((LANES, width), 1) // BS + n * PER)
        force = force + ops * (dot(stress[0], copies) + dot(stress[1], copies) + dot(stress[2], copies))
    placer = jnp.transpose(member)[:BS].astype(jnp.bfloat16)
    return folded(dot(placer, stacked(folded(force, BS), 1)), BS)


def own_body(strains, field_ref, got_ref, out_ref):
    out_ref[...] = own_part(strains, field_ref[...], got_ref)


def own_of(field, got, strains):
    return pl.pallas_call(
        functools.partial(own_body, strains),
        compiler_params=LIMIT,
        cost_estimate=WORK,
        out_shape=jax.ShapeDtypeStruct(field.shape, jnp.float32),
    )(field, got)


def own_spread_body(strains, last_ref, got_ref, rest_ref, wide_hbm, cols_ref, *refs):
    down_ref, here_ref, up_ref, field_ref, returned_ref, wide_ref, arrival = refs
    steps = field_ref.shape[0] // ROWS
    part = ROWS * BS
    loads = [
        pltpu.make_async_copy(
            wide_hbm.at[pl.ds(n * part, part)], wide_ref.at[pl.ds(n * part, part)], arrival.at[n]
        )
        for n in range(steps)
    ]
    for load in loads:
        load.start()
    field_ref[...] = (rest_ref[...] + own_part(strains, last_ref[...], got_ref)) * SCALE
    for step, load in enumerate(loads):
        load.wait()
        spread_rows(step, step, field_ref, wide_ref, returned_ref)
    spread_messages(field_ref, cols_ref, down_ref, here_ref, up_ref, returned_ref)


def own_spread_of(last, got, strains, rest, wide, cols_row):
    rows = last.shape[0]
    message = jax.ShapeDtypeStruct((rows, 2 * BS), jnp.float32)
    vector = jax.ShapeDtypeStruct(last.shape, jnp.float32)
    return pl.pallas_call(
        functools.partial(own_spread_body, strains),
        in_specs=[
            whole(last.shape),
            whole(got.shape),
            whole(rest.shape),
            pl.BlockSpec(memory_space=pl.ANY),
            whole(cols_row.shape),
        ],
        out_specs=[whole(v.shape) for v in (message, vector, message, vector)],
        compiler_params=LIMIT,
        cost_estimate=WORK,
        out_shape=[message, vector, message, vector],
        scratch_shapes=[
            pltpu.VMEM((rows, K * BS), jnp.float32),
            pltpu.VMEM(wide.shape, jnp.float32),
            pltpu.SemaphoreType.DMA((rows // ROWS,)),
        ],
    )(last, got, rest, pltpu.with_memory_space_constraint(wide, pltpu.HBM), cols_row)


def finish_body(ends_ref, got_ref, w0_ref, w1_ref, w2_ref, *refs):
    rest_ref, here_ref, lower_ref, upper_ref, solution_ref, residual_ref = refs
    total = jnp.sum(got_ref[...], axis=0, keepdims=True)
    moments = [total[:, n : n + 1] for n in range(2 * ITERS)]
    x_coef, r_coef = conjugate_coefficients(moments)
    lower, upper = arrived(ends_ref, lower_ref[:, BS:], upper_ref[:, BS:])
    w3 = (rest_ref[...] + here_ref[...] + (lower + upper)) * SCALE
    basis = [w0_ref[...], w1_ref[...], w2_ref[...], w3]
    solution_ref[...] = combine(x_coef, basis)
    residual_ref[...] = combine(r_coef, basis)


def ring(shard, axis, by):
    count = lax.axis_size(axis)
    return lax.ppermute(shard, axis, [(i, (i + by) % count) for i in range(count)])


def square(coefs):
    out = [0.0] * (2 * len(coefs) - 1)
    for i, a in enumerate(coefs):
        for j, b in enumerate(coefs):
            out[i + j] = out[i + j] + a * b
    return out


def plus(a, b):
    size = max(len(a), len(b))
    a, b = (list(v) + [0.0] * (size - len(v)) for v in (a, b))
    return [u + v for u, v in zip(a, b)]


def times(scalar, coefs):
    return [scalar * v for v in coefs]


def conjugate_coefficients(moments):
    x, r, p = [0.0], [1.0], [1.0]
    rr = moments[0]
    for step in range(ITERS):
        sq = square(p)
        bottom = sum(
            u * (moments[n + 1] * (1.0 / SCALE) + SHIFT * moments[n]) for n, u in enumerate(sq)
        )
        alpha = rr / bottom
        x = plus(x, times(alpha, p))
        image = plus([0.0] + times(1.0 / SCALE, p), times(SHIFT, p))
        r = plus(r, times(-alpha, image))
        if step < ITERS - 1:
            new = sum(u * moments[n] for n, u in enumerate(square(r)))
            p = plus(r, times(new / rr, p))
            rr = new
    return x, r


def combine(coefs, basis):
    total = coefs[0] * basis[0]
    for a, v in zip(coefs[1:], basis[1:]):
        total = total + a * v
    return total


def per_device(elem_ops, elem_stiff, owner, row_slot, couplings, coupling_cols, mass, rhs):
    rows_here = rhs.shape[0]
    owners = lax.axis_size("dev")
    count, strains, _ = elem_ops.shape
    capacity = 2 * count // owners
    slots = owners * capacity
    packed = pack(
        elem_ops.reshape(count, strains * BS), elem_stiff.T, owner.T, row_slot[None, :], slots, capacity
    )
    got = lax.all_to_all(
        packed, "dev", split_axis=0, concat_axis=0, tiled=True
    ).reshape(slots, -1)
    cols_row = coupling_cols.T.reshape(1, K * rows_here)
    wide = widened(couplings)
    place = lax.axis_index("group")
    ends = jnp.stack([place, lax.axis_size("group") - 1 - place]).astype(jnp.int32)

    def sent(down, here, up):
        return here, ring(up, "group", 1), ring(down, "group", -1)

    here, lower, upper = sent(*spread_of(rhs, wide, cols_row))
    rest = cross_of(ends, lower, rhs, upper, wide, coupling_cols, mass, here)
    *messages, w1 = own_spread_of(rhs, got, strains, rest, wide, cols_row)
    here, lower, upper = sent(*messages)
    own = own_of(w1, got, strains)
    w2 = cross_of(ends, lower, w1, upper, wide, coupling_cols, mass, here, own)
    lower, upper = ring(w2, "group", 1), ring(w2, "group", -1)
    own = own_of(w2, got, strains)
    members = lax.axis_size("group") * lax.axis_size("dev")
    rest, parts = cross_of(
        ends, lower, w2, upper, wide, coupling_cols, mass, own, earlier=(rhs, w1), members=members
    )
    got_parts = lax.all_to_all(parts, EVERY, 0, 0, tiled=True)
    here, lower, upper = sent(*spread_of(w2, wide, cols_row))
    operands = (ends, got_parts, rhs, w1, w2, rest, here, lower, upper)
    result = jax.ShapeDtypeStruct(rhs.shape, jnp.float32)
    return tuple(
        pl.pallas_call(
            finish_body,
            in_specs=[pl.BlockSpec(memory_space=pltpu.SMEM)]
            + [whole(v.shape) for v in operands[1:]],
            out_specs=[whole(rhs.shape)] * 2,
            compiler_params=LIMIT,
            out_shape=[result, result],
        )(*operands)
    )


def solution(mesh):
    placed = (
        P(EVERY, None, None),
        P(EVERY, None),
        P(EVERY, None),
        P(EVERY),
        P(EVERY, None, None, None),
        P(EVERY, None),
        P(EVERY, None),
        P(EVERY, None),
    )
    return jax.shard_map(
        per_device,
        mesh=mesh,
        in_specs=placed,
        out_specs=(P(EVERY, None), P(EVERY, None)),
        check_vma=False,
    )
```

```python
import functools

import jax
import jax.numpy as jnp
from jax import lax
from jax.experimental import pallas as pl
from jax.experimental.pallas import tpu as pltpu
from jax.sharding import PartitionSpec as P

BS = 64
K = 4
LANES = 128
GROUP = 8
ROWS = 64
PART = 16
PER = 4
ITERS = 3
SHIFT = 4.0
SCALE = 0.125
LIMIT = pltpu.CompilerParams(vmem_limit_bytes=16 * 1024 * 1024)
WORK = pl.CostEstimate(flops=2_000_000_000, transcendentals=0, bytes_accessed=4_194_304)
EVERY = ("group", "dev")


def pieces(x):
    high = x.astype(jnp.bfloat16).astype(jnp.float32)
    rest = x - high
    middle = rest.astype(jnp.bfloat16).astype(jnp.float32)
    return high, middle, rest - middle


def stacked(x, axis):
    return jnp.concatenate(pieces(x), axis=axis).astype(jnp.bfloat16)


def folded(x, width):
    total = x[:, :width]
    for n in range(1, x.shape[1] // width):
        total = total + x[:, n * width : (n + 1) * width]
    return total


def iota(shape, dim):
    return lax.broadcasted_iota(jnp.int32, shape, dim)


def onehot(mask):
    return jnp.where(mask, 1.0, 0.0).astype(jnp.bfloat16)


def dot(a, b):
    return jnp.dot(a, b, preferred_element_type=jnp.float32)


def dot_nt(a, b):
    return lax.dot_general(a, b, (((1,), (1,)), ((), ())), preferred_element_type=jnp.float32)


def whole(shape):
    return pl.BlockSpec(shape, lambda *_: (0,) * len(shape))


def widen_body(blocks_ref, out_ref):
    for r in range(GROUP):
        out_ref[r * BS : (r + 1) * BS, :] = jnp.concatenate(
            [blocks_ref[r, k] for k in range(K)], axis=1
        )


def widened(couplings):
    rows = couplings.shape[0]
    return pl.pallas_call(
        widen_body,
        grid=(rows // GROUP,),
        in_specs=[pl.BlockSpec((GROUP, K, BS, BS), lambda n: (n, 0, 0, 0))],
        out_specs=pl.BlockSpec((GROUP * BS, K * BS), lambda n: (n, 0)),
        compiler_params=LIMIT,
        cost_estimate=WORK,
        out_shape=jax.ShapeDtypeStruct((rows * BS, K * BS), jnp.float32),
    )(pltpu.with_memory_space_constraint(couplings, pltpu.HBM))


def spread_rows(size, step, block, field_ref, wide_ref, returned_ref):
    for g in range(size // GROUP):
        base = step * size + g * GROUP
        base = base if isinstance(base, int) else pl.multiple_of(base, GROUP)
        tall = jnp.transpose(field_ref[pl.ds(base, GROUP), :])
        found = []
        for r in range(GROUP):
            at = (block * size + g * GROUP + r) * BS
            found.append(
                jnp.sum(wide_ref[pl.ds(at, BS), :] * tall[:, r : r + 1], axis=0, keepdims=True)
            )
        returned_ref[pl.ds(base, GROUP), :] = jnp.concatenate(found, axis=0)


def spread_messages(field_ref, cols_ref, down_ref, here_ref, up_ref, returned_ref):
    returned = returned_ref[...]
    tall = jnp.concatenate([returned[:, k * BS : (k + 1) * BS] for k in range(K)], axis=0)
    rows = field_ref.shape[0]
    shape = (3 * rows, tall.shape[0])
    placer = onehot(iota(shape, 0) == cols_ref[...])
    spread = folded(dot(placer, stacked(tall, 1)), BS)
    field = field_ref[...]
    down_ref[...] = jnp.concatenate([field, spread[:rows]], axis=1)
    here_ref[...] = spread[rows : 2 * rows]
    up_ref[...] = jnp.concatenate([field, spread[2 * rows :]], axis=1)


def spread_body(field_ref, wide_ref, cols_ref, down_ref, here_ref, up_ref, returned_ref):
    step = pl.program_id(0)
    spread_rows(ROWS, step, 0, field_ref, wide_ref, returned_ref)

    @pl.when(step == pl.num_programs(0) - 1)
    def _():
        spread_messages(field_ref, cols_ref, down_ref, here_ref, up_ref, returned_ref)


def spread_of(field, wide, cols_row):
    rows = field.shape[0]
    message = jax.ShapeDtypeStruct((rows, 2 * BS), jnp.float32)
    return pl.pallas_call(
        spread_body,
        grid=(rows // ROWS,),
        in_specs=[
            whole(field.shape),
            pl.BlockSpec((ROWS * BS, K * BS), lambda n: (n, 0)),
            whole(cols_row.shape),
        ],
        out_specs=[whole((rows, 2 * BS)), whole((rows, BS)), whole((rows, 2 * BS))],
        compiler_params=LIMIT,
        cost_estimate=WORK,
        out_shape=[message, jax.ShapeDtypeStruct(field.shape, jnp.float32), message],
        scratch_shapes=[pltpu.VMEM((rows, K * BS), jnp.float32)],
    )(field, wide, cols_row)


def arrived(ends_ref, lower, upper):
    return jnp.where(ends_ref[0] > 0, lower, 0.0), jnp.where(ends_ref[1] > 0, upper, 0.0)


def cross_body(extra, last, *refs):
    ends_ref, lower_ref, field_ref, upper_ref, wide_ref, cols_ref, mass_ref = refs[:7]
    added, rest = refs[7 : 7 + extra], refs[7 + extra :]
    if last:
        *earlier, out_ref, sums_ref, near_ref, twice_ref = rest
        out_refs = (out_ref, sums_ref)
    else:
        *out_refs, near_ref = rest
    step = pl.program_id(0)
    rows = field_ref.shape[0]

    @pl.when(step == 0)
    def _():
        lower, upper = arrived(ends_ref, lower_ref[:, :BS], upper_ref[:, :BS])
        extended = stacked(jnp.concatenate([lower, field_ref[...], upper], axis=0), 1)
        lanes = iota((rows, 3 * rows), 1)
        picker = [onehot(lanes == cols_ref[:, k : k + 1]) for k in range(K)]
        near_ref[...] = jnp.concatenate([folded(dot(p, extended), BS) for p in picker], axis=1)

    same = iota((BS, BS), 0) == iota((BS, BS), 1)
    for g in range(ROWS // GROUP):
        base = pl.multiple_of(step * ROWS + g * GROUP, GROUP)
        here = pl.ds(base, GROUP)
        near = near_ref[here, :]
        found = []
        for r in range(GROUP):
            at = (g * GROUP + r) * BS
            product = wide_ref[at : at + BS, :] * near[r : r + 1, :]
            total = jnp.sum(product, axis=1, keepdims=True)
            found.append(jnp.sum(jnp.where(same, total, 0.0), axis=0, keepdims=True))
        cross = jnp.concatenate(found, axis=0)
        image = cross + (mass_ref[here, :] - SHIFT) * field_ref[here, :]
        for ref in added:
            image = image + ref[here, :]
        if last:
            out_refs[0][here, :] = image
            twice_ref[here, :] = image + cross
        else:
            lower, upper = arrived(ends_ref, lower_ref[here, BS:], upper_ref[here, BS:])
            image = image + (lower + upper)
            out_refs[0][here, :] = image * SCALE if extra == 2 else image

    if last:

        @pl.when(step == pl.num_programs(0) - 1)
        def _():
            fourth = twice_ref[...] * SCALE
            basis = [ref[...] for ref in earlier] + [field_ref[...], fourth]
            lane = iota((1, LANES), 1)
            row = jnp.zeros((1, LANES), jnp.float32)
            for n in range(2 * ITERS):
                product = basis[n // 2] * basis[n - n // 2]
                total = jnp.sum(jnp.sum(product, axis=0, keepdims=True), axis=1, keepdims=True)
                row = jnp.where(lane == n, total, row)
            out_refs[1][...] = jnp.broadcast_to(row, out_refs[1].shape)


def cross_of(ends, lower, field, upper, wide, cols, mass, *added, earlier=(), members=0):
    rows = field.shape[0]
    last = len(earlier) > 0
    vector = jax.ShapeDtypeStruct(field.shape, jnp.float32)
    results = [vector] + [jax.ShapeDtypeStruct((members, LANES), jnp.float32)] * last
    found = pl.pallas_call(
        functools.partial(cross_body, len(added), last),
        grid=(rows // ROWS,),
        in_specs=[
            pl.BlockSpec(memory_space=pltpu.SMEM),
            whole(lower.shape),
            whole(field.shape),
            whole(upper.shape),
            pl.BlockSpec((ROWS * BS, K * BS), lambda n: (n, 0)),
            whole(cols.shape),
            *[whole(field.shape)] * (1 + len(added) + len(earlier)),
        ],
        out_specs=[whole(v.shape) for v in results],
        compiler_params=LIMIT,
        cost_estimate=WORK,
        out_shape=results,
        scratch_shapes=[pltpu.VMEM((rows, K * BS), jnp.float32)]
        + [pltpu.VMEM(field.shape, jnp.float32)] * last,
    )(ends, lower, field, upper, wide, cols, mass, *added, *earlier)
    return found if last else found[0]


def pack_body(capacity, ops_ref, stiff_ref, owner_ref, slot_ref, out_ref):
    owners, _, width = out_ref.shape
    slots = owners * capacity
    strains, count = stiff_ref.shape
    owner = owner_ref[...]
    across = jnp.broadcast_to(owner.astype(jnp.float32), (count, count))
    earlier = (across == jnp.transpose(across)) & (
        iota((count, count), 0) < iota((count, count), 1)
    )
    rank = jnp.sum(jnp.where(earlier, 1.0, 0.0), axis=0, keepdims=True).astype(jnp.int32)
    picker = onehot(iota((slots, count), 0) == owner * capacity + rank)
    body = strains * BS
    for at in range(0, body, 4 * LANES):
        lanes = slice(at, at + 4 * LANES)
        out_ref[:, :, lanes] = (
            dot(picker, ops_ref[:, lanes]).reshape(owners, capacity, -1).astype(jnp.bfloat16)
        )
    tail = jnp.concatenate(
        [
            stiff_ref[...].astype(jnp.float32),
            slot_ref[...].astype(jnp.float32),
            jnp.zeros((width - body - strains - 1, count), jnp.float32),
        ],
        axis=0,
    )
    ends = dot_nt(picker, tail.astype(jnp.bfloat16))
    out_ref[:, :, body:] = ends.reshape(owners, capacity, -1).astype(jnp.bfloat16)


def pack(ops, stiff, owner, slot, slots, capacity):
    body = ops.shape[1]
    return pl.pallas_call(
        functools.partial(pack_body, capacity),
        compiler_params=LIMIT,
        cost_estimate=WORK,
        out_shape=jax.ShapeDtypeStruct((slots // capacity, capacity, body + LANES), jnp.bfloat16),
    )(ops, *(pltpu.with_memory_space_constraint(v, pltpu.HBM) for v in (stiff, owner, slot)))


def own_part(strains, field, got_ref):
    slots = got_ref.shape[0]
    tail = got_ref[:, strains * BS :].astype(jnp.float32)
    rows = tail[:, strains : strains + 1].astype(jnp.int32)
    member = jnp.where(iota((slots, LANES), 1) == rows, 1.0, 0.0)
    local = folded(dot(member[:, :BS].astype(jnp.bfloat16), stacked(field, 1)), BS)
    pair = jnp.concatenate([local] * PER, axis=1)
    width = PER * BS
    turn = iota((slots, LANES), 1) // PER
    sums = onehot(iota((width, LANES), 1) % PER == iota((width, LANES), 0) // BS)
    copies = onehot(iota((LANES, width), 0) % PER == iota((LANES, width), 1) // BS)
    strain = jnp.zeros((slots, LANES), jnp.float32)
    for n in range(strains // PER):
        ops = got_ref[:, n * width : (n + 1) * width].astype(jnp.float32)
        high, middle, low = (dot(p.astype(jnp.bfloat16), sums) for p in pieces(ops * pair))
        strain = jnp.where(turn == n, high + middle + low, strain)
    stress = pieces(strain * tail)
    force = jnp.zeros((slots, width), jnp.float32)
    for n in range(strains // PER):
        ops = got_ref[:, n * width : (n + 1) * width].astype(jnp.float32)
        high, middle, low = (
            dot(jnp.where(turn == n, p, 0.0).astype(jnp.bfloat16), copies) for p in stress
        )
        force = force + ops * (high + middle + low)
    placer = jnp.transpose(member)[:BS].astype(jnp.bfloat16)
    return folded(dot(placer, stacked(folded(force, BS), 1)), BS)


def own_body(strains, field_ref, got_ref, out_ref):
    out_ref[...] = own_part(strains, field_ref[...], got_ref)


def own_of(field, got, strains):
    return pl.pallas_call(
        functools.partial(own_body, strains),
        compiler_params=LIMIT,
        cost_estimate=WORK,
        out_shape=jax.ShapeDtypeStruct(field.shape, jnp.float32),
    )(field, got)


def own_spread_body(strains, last_ref, got_ref, rest_ref, wide_hbm, cols_ref, *refs):
    down_ref, here_ref, up_ref, field_ref, returned_ref, wide_ref, arrival = refs
    steps = field_ref.shape[0] // PART
    part = PART * BS
    loads = [
        pltpu.make_async_copy(
            wide_hbm.at[pl.ds(n * part, part)], wide_ref.at[pl.ds(n * part, part)], arrival.at[n]
        )
        for n in range(steps)
    ]
    for load in loads:
        load.start()
    field_ref[...] = (rest_ref[...] + own_part(strains, last_ref[...], got_ref)) * SCALE
    for step, load in enumerate(loads):
        load.wait()
        spread_rows(PART, step, step, field_ref, wide_ref, returned_ref)
    spread_messages(field_ref, cols_ref, down_ref, here_ref, up_ref, returned_ref)


def own_spread_of(last, got, strains, rest, wide, cols_row):
    rows = last.shape[0]
    message = jax.ShapeDtypeStruct((rows, 2 * BS), jnp.float32)
    vector = jax.ShapeDtypeStruct(last.shape, jnp.float32)
    return pl.pallas_call(
        functools.partial(own_spread_body, strains),
        in_specs=[
            whole(last.shape),
            whole(got.shape),
            whole(rest.shape),
            pl.BlockSpec(memory_space=pl.ANY),
            whole(cols_row.shape),
        ],
        out_specs=[whole(v.shape) for v in (message, vector, message, vector)],
        compiler_params=LIMIT,
        cost_estimate=WORK,
        out_shape=[message, vector, message, vector],
        scratch_shapes=[
            pltpu.VMEM((rows, K * BS), jnp.float32),
            pltpu.VMEM(wide.shape, jnp.float32),
            pltpu.SemaphoreType.DMA((rows // PART,)),
        ],
    )(last, got, rest, pltpu.with_memory_space_constraint(wide, pltpu.HBM), cols_row)


def finish_body(ends_ref, got_ref, w0_ref, w1_ref, w2_ref, *refs):
    rest_ref, here_ref, lower_ref, upper_ref, solution_ref, residual_ref = refs
    total = jnp.sum(got_ref[...], axis=0, keepdims=True)
    moments = [total[:, n : n + 1] for n in range(2 * ITERS)]
    x_coef, r_coef = conjugate_coefficients(moments)
    lower, upper = arrived(ends_ref, lower_ref[:, BS:], upper_ref[:, BS:])
    w3 = (rest_ref[...] + here_ref[...] + (lower + upper)) * SCALE
    basis = [w0_ref[...], w1_ref[...], w2_ref[...], w3]
    solution_ref[...] = combine(x_coef, basis)
    residual_ref[...] = combine(r_coef, basis)


def ring(shard, axis, by):
    count = lax.axis_size(axis)
    return lax.ppermute(shard, axis, [(i, (i + by) % count) for i in range(count)])


def square(coefs):
    out = [0.0] * (2 * len(coefs) - 1)
    for i, a in enumerate(coefs):
        for j, b in enumerate(coefs):
            out[i + j] = out[i + j] + a * b
    return out


def plus(a, b):
    size = max(len(a), len(b))
    a, b = (list(v) + [0.0] * (size - len(v)) for v in (a, b))
    return [u + v for u, v in zip(a, b)]


def times(scalar, coefs):
    return [scalar * v for v in coefs]


def conjugate_coefficients(moments):
    x, r, p = [0.0], [1.0], [1.0]
    rr = moments[0]
    for step in range(ITERS):
        sq = square(p)
        bottom = sum(
            u * (moments[n + 1] * (1.0 / SCALE) + SHIFT * moments[n]) for n, u in enumerate(sq)
        )
        alpha = rr / bottom
        x = plus(x, times(alpha, p))
        image = plus([0.0] + times(1.0 / SCALE, p), times(SHIFT, p))
        r = plus(r, times(-alpha, image))
        if step < ITERS - 1:
            new = sum(u * moments[n] for n, u in enumerate(square(r)))
            p = plus(r, times(new / rr, p))
            rr = new
    return x, r


def combine(coefs, basis):
    total = coefs[0] * basis[0]
    for a, v in zip(coefs[1:], basis[1:]):
        total = total + a * v
    return total


def per_device(elem_ops, elem_stiff, owner, row_slot, couplings, coupling_cols, mass, rhs):
    rows_here = rhs.shape[0]
    owners = lax.axis_size("dev")
    count, strains, _ = elem_ops.shape
    capacity = 2 * count // owners
    slots = owners * capacity
    packed = pack(
        elem_ops.reshape(count, strains * BS), elem_stiff.T, owner.T, row_slot[None, :], slots, capacity
    )
    got = lax.all_to_all(
        packed, "dev", split_axis=0, concat_axis=0, tiled=True
    ).reshape(slots, -1)
    cols_row = coupling_cols.T.reshape(1, K * rows_here)
    wide = widened(couplings)
    place = lax.axis_index("group")
    ends = jnp.stack([place, lax.axis_size("group") - 1 - place]).astype(jnp.int32)

    def sent(down, here, up):
        return here, ring(up, "group", 1), ring(down, "group", -1)

    here, lower, upper = sent(*spread_of(rhs, wide, cols_row))
    rest = cross_of(ends, lower, rhs, upper, wide, coupling_cols, mass, here)
    *messages, w1 = own_spread_of(rhs, got, strains, rest, wide, cols_row)
    here, lower, upper = sent(*messages)
    own = own_of(w1, got, strains)
    w2 = cross_of(ends, lower, w1, upper, wide, coupling_cols, mass, here, own)
    lower, upper = ring(w2, "group", 1), ring(w2, "group", -1)
    own = own_of(w2, got, strains)
    members = lax.axis_size("group") * lax.axis_size("dev")
    rest, parts = cross_of(
        ends, lower, w2, upper, wide, coupling_cols, mass, own, earlier=(rhs, w1), members=members
    )
    got_parts = lax.all_to_all(parts, EVERY, 0, 0, tiled=True)
    here, lower, upper = sent(*spread_of(w2, wide, cols_row))
    operands = (ends, got_parts, rhs, w1, w2, rest, here, lower, upper)
    result = jax.ShapeDtypeStruct(rhs.shape, jnp.float32)
    return tuple(
        pl.pallas_call(
            finish_body,
            in_specs=[pl.BlockSpec(memory_space=pltpu.SMEM)]
            + [whole(v.shape) for v in operands[1:]],
            out_specs=[whole(rhs.shape)] * 2,
            compiler_params=LIMIT,
            out_shape=[result, result],
        )(*operands)
    )


def solution(mesh):
    placed = (
        P(EVERY, None, None),
        P(EVERY, None),
        P(EVERY, None),
        P(EVERY),
        P(EVERY, None, None, None),
        P(EVERY, None),
        P(EVERY, None),
        P(EVERY, None),
    )
    return jax.shard_map(
        per_device,
        mesh=mesh,
        in_specs=placed,
        out_specs=(P(EVERY, None), P(EVERY, None)),
        check_vma=False,
    )
```

```python
import functools

import jax
import jax.numpy as jnp
from jax import lax
from jax.experimental import pallas as pl
from jax.experimental.pallas import tpu as pltpu
from jax.sharding import PartitionSpec as P

BS = 64
K = 4
LANES = 128
GROUP = 8
ROWS = 64
PART = 8
PER = 4
ITERS = 3
SHIFT = 4.0
SCALE = 0.125
LIMIT = pltpu.CompilerParams(vmem_limit_bytes=16 * 1024 * 1024)
WORK = pl.CostEstimate(flops=2_000_000_000, transcendentals=0, bytes_accessed=4_194_304)
EVERY = ("group", "dev")


def pieces(x):
    high = x.astype(jnp.bfloat16).astype(jnp.float32)
    rest = x - high
    middle = rest.astype(jnp.bfloat16).astype(jnp.float32)
    return high, middle, rest - middle


def stacked(x, axis):
    return jnp.concatenate(pieces(x), axis=axis).astype(jnp.bfloat16)


def folded(x, width):
    total = x[:, :width]
    for n in range(1, x.shape[1] // width):
        total = total + x[:, n * width : (n + 1) * width]
    return total


def iota(shape, dim):
    return lax.broadcasted_iota(jnp.int32, shape, dim)


def onehot(mask):
    return jnp.where(mask, 1.0, 0.0).astype(jnp.bfloat16)


def dot(a, b):
    return jnp.dot(a, b, preferred_element_type=jnp.float32)


def dot_nt(a, b):
    return lax.dot_general(a, b, (((1,), (1,)), ((), ())), preferred_element_type=jnp.float32)


def whole(shape):
    return pl.BlockSpec(shape, lambda *_: (0,) * len(shape))


def widen_body(blocks_ref, out_ref):
    for r in range(GROUP):
        out_ref[r * BS : (r + 1) * BS, :] = jnp.concatenate(
            [blocks_ref[r, k] for k in range(K)], axis=1
        )


def widened(couplings):
    rows = couplings.shape[0]
    return pl.pallas_call(
        widen_body,
        grid=(rows // GROUP,),
        in_specs=[pl.BlockSpec((GROUP, K, BS, BS), lambda n: (n, 0, 0, 0))],
        out_specs=pl.BlockSpec((GROUP * BS, K * BS), lambda n: (n, 0)),
        compiler_params=LIMIT,
        cost_estimate=WORK,
        out_shape=jax.ShapeDtypeStruct((rows * BS, K * BS), jnp.float32),
    )(pltpu.with_memory_space_constraint(couplings, pltpu.HBM))


def spread_rows(size, step, block, field_ref, wide_ref, returned_ref):
    for g in range(size // GROUP):
        base = step * size + g * GROUP
        base = base if isinstance(base, int) else pl.multiple_of(base, GROUP)
        tall = jnp.transpose(field_ref[pl.ds(base, GROUP), :])
        found = []
        for r in range(GROUP):
            at = (block * size + g * GROUP + r) * BS
            found.append(
                jnp.sum(wide_ref[pl.ds(at, BS), :] * tall[:, r : r + 1], axis=0, keepdims=True)
            )
        returned_ref[pl.ds(base, GROUP), :] = jnp.concatenate(found, axis=0)


def spread_messages(field_ref, cols_ref, down_ref, here_ref, up_ref, returned_ref):
    returned = returned_ref[...]
    tall = jnp.concatenate([returned[:, k * BS : (k + 1) * BS] for k in range(K)], axis=0)
    rows = field_ref.shape[0]
    shape = (3 * rows, tall.shape[0])
    placer = onehot(iota(shape, 0) == cols_ref[...])
    spread = folded(dot(placer, stacked(tall, 1)), BS)
    field = field_ref[...]
    down_ref[...] = jnp.concatenate([field, spread[:rows]], axis=1)
    here_ref[...] = spread[rows : 2 * rows]
    up_ref[...] = jnp.concatenate([field, spread[2 * rows :]], axis=1)


def spread_body(field_ref, wide_ref, cols_ref, down_ref, here_ref, up_ref, returned_ref):
    step = pl.program_id(0)
    spread_rows(ROWS, step, 0, field_ref, wide_ref, returned_ref)

    @pl.when(step == pl.num_programs(0) - 1)
    def _():
        spread_messages(field_ref, cols_ref, down_ref, here_ref, up_ref, returned_ref)


def spread_of(field, wide, cols_row):
    rows = field.shape[0]
    message = jax.ShapeDtypeStruct((rows, 2 * BS), jnp.float32)
    return pl.pallas_call(
        spread_body,
        grid=(rows // ROWS,),
        in_specs=[
            whole(field.shape),
            pl.BlockSpec((ROWS * BS, K * BS), lambda n: (n, 0)),
            whole(cols_row.shape),
        ],
        out_specs=[whole((rows, 2 * BS)), whole((rows, BS)), whole((rows, 2 * BS))],
        compiler_params=LIMIT,
        cost_estimate=WORK,
        out_shape=[message, jax.ShapeDtypeStruct(field.shape, jnp.float32), message],
        scratch_shapes=[pltpu.VMEM((rows, K * BS), jnp.float32)],
    )(field, wide, cols_row)


def arrived(ends_ref, lower, upper):
    return jnp.where(ends_ref[0] > 0, lower, 0.0), jnp.where(ends_ref[1] > 0, upper, 0.0)


def cross_body(extra, last, *refs):
    ends_ref, lower_ref, field_ref, upper_ref, wide_ref, cols_ref, mass_ref = refs[:7]
    added, rest = refs[7 : 7 + extra], refs[7 + extra :]
    if last:
        *earlier, out_ref, sums_ref, near_ref, twice_ref = rest
        out_refs = (out_ref, sums_ref)
    else:
        *out_refs, near_ref = rest
    step = pl.program_id(0)
    rows = field_ref.shape[0]

    @pl.when(step == 0)
    def _():
        lower, upper = arrived(ends_ref, lower_ref[:, :BS], upper_ref[:, :BS])
        extended = stacked(jnp.concatenate([lower, field_ref[...], upper], axis=0), 1)
        lanes = iota((rows, 3 * rows), 1)
        picker = [onehot(lanes == cols_ref[:, k : k + 1]) for k in range(K)]
        near_ref[...] = jnp.concatenate([folded(dot(p, extended), BS) for p in picker], axis=1)

    same = iota((BS, BS), 0) == iota((BS, BS), 1)
    for g in range(ROWS // GROUP):
        base = pl.multiple_of(step * ROWS + g * GROUP, GROUP)
        here = pl.ds(base, GROUP)
        near = near_ref[here, :]
        found = []
        for r in range(GROUP):
            at = (g * GROUP + r) * BS
            product = wide_ref[at : at + BS, :] * near[r : r + 1, :]
            total = jnp.sum(product, axis=1, keepdims=True)
            found.append(jnp.sum(jnp.where(same, total, 0.0), axis=0, keepdims=True))
        cross = jnp.concatenate(found, axis=0)
        image = cross + (mass_ref[here, :] - SHIFT) * field_ref[here, :]
        for ref in added:
            image = image + ref[here, :]
        if last:
            out_refs[0][here, :] = image
            twice_ref[here, :] = image + cross
        else:
            lower, upper = arrived(ends_ref, lower_ref[here, BS:], upper_ref[here, BS:])
            image = image + (lower + upper)
            out_refs[0][here, :] = image * SCALE if extra == 2 else image

    if last:

        @pl.when(step == pl.num_programs(0) - 1)
        def _():
            fourth = twice_ref[...] * SCALE
            basis = [ref[...] for ref in earlier] + [field_ref[...], fourth]
            lane = iota((1, LANES), 1)
            row = jnp.zeros((1, LANES), jnp.float32)
            for n in range(2 * ITERS):
                product = basis[n // 2] * basis[n - n // 2]
                total = jnp.sum(jnp.sum(product, axis=0, keepdims=True), axis=1, keepdims=True)
                row = jnp.where(lane == n, total, row)
            out_refs[1][...] = jnp.broadcast_to(row, out_refs[1].shape)


def cross_of(ends, lower, field, upper, wide, cols, mass, *added, earlier=(), members=0):
    rows = field.shape[0]
    last = len(earlier) > 0
    vector = jax.ShapeDtypeStruct(field.shape, jnp.float32)
    results = [vector] + [jax.ShapeDtypeStruct((members, LANES), jnp.float32)] * last
    found = pl.pallas_call(
        functools.partial(cross_body, len(added), last),
        grid=(rows // ROWS,),
        in_specs=[
            pl.BlockSpec(memory_space=pltpu.SMEM),
            whole(lower.shape),
            whole(field.shape),
            whole(upper.shape),
            pl.BlockSpec((ROWS * BS, K * BS), lambda n: (n, 0)),
            whole(cols.shape),
            *[whole(field.shape)] * (1 + len(added) + len(earlier)),
        ],
        out_specs=[whole(v.shape) for v in results],
        compiler_params=LIMIT,
        cost_estimate=WORK,
        out_shape=results,
        scratch_shapes=[pltpu.VMEM((rows, K * BS), jnp.float32)]
        + [pltpu.VMEM(field.shape, jnp.float32)] * last,
    )(ends, lower, field, upper, wide, cols, mass, *added, *earlier)
    return found if last else found[0]


def pack_body(capacity, ops_ref, stiff_ref, owner_ref, slot_ref, out_ref):
    owners, _, width = out_ref.shape
    slots = owners * capacity
    strains, count = stiff_ref.shape
    owner = owner_ref[...]
    across = jnp.broadcast_to(owner.astype(jnp.float32), (count, count))
    earlier = (across == jnp.transpose(across)) & (
        iota((count, count), 0) < iota((count, count), 1)
    )
    rank = jnp.sum(jnp.where(earlier, 1.0, 0.0), axis=0, keepdims=True).astype(jnp.int32)
    picker = onehot(iota((slots, count), 0) == owner * capacity + rank)
    body = strains * BS
    for at in range(0, body, 4 * LANES):
        lanes = slice(at, at + 4 * LANES)
        out_ref[:, :, lanes] = (
            dot(picker, ops_ref[:, lanes]).reshape(owners, capacity, -1).astype(jnp.bfloat16)
        )
    tail = jnp.concatenate(
        [
            stiff_ref[...].astype(jnp.float32),
            slot_ref[...].astype(jnp.float32),
            jnp.zeros((width - body - strains - 1, count), jnp.float32),
        ],
        axis=0,
    )
    ends = dot_nt(picker, tail.astype(jnp.bfloat16))
    out_ref[:, :, body:] = ends.reshape(owners, capacity, -1).astype(jnp.bfloat16)


def pack(ops, stiff, owner, slot, slots, capacity):
    body = ops.shape[1]
    return pl.pallas_call(
        functools.partial(pack_body, capacity),
        compiler_params=LIMIT,
        cost_estimate=WORK,
        out_shape=jax.ShapeDtypeStruct((slots // capacity, capacity, body + LANES), jnp.bfloat16),
    )(ops, *(pltpu.with_memory_space_constraint(v, pltpu.HBM) for v in (stiff, owner, slot)))


def own_part(strains, field, got_ref):
    slots = got_ref.shape[0]
    tail = got_ref[:, strains * BS :].astype(jnp.float32)
    rows = tail[:, strains : strains + 1].astype(jnp.int32)
    member = jnp.where(iota((slots, LANES), 1) == rows, 1.0, 0.0)
    local = folded(dot(member[:, :BS].astype(jnp.bfloat16), stacked(field, 1)), BS)
    pair = jnp.concatenate([local] * PER, axis=1)
    width = PER * BS
    turn = iota((slots, LANES), 1) // PER
    sums = onehot(iota((width, LANES), 1) % PER == iota((width, LANES), 0) // BS)
    copies = onehot(iota((LANES, width), 0) % PER == iota((LANES, width), 1) // BS)
    strain = jnp.zeros((slots, LANES), jnp.float32)
    for n in range(strains // PER):
        ops = got_ref[:, n * width : (n + 1) * width].astype(jnp.float32)
        high, middle, low = (dot(p.astype(jnp.bfloat16), sums) for p in pieces(ops * pair))
        strain = jnp.where(turn == n, high + middle + low, strain)
    stress = pieces(strain * tail)
    force = jnp.zeros((slots, width), jnp.float32)
    for n in range(strains // PER):
        ops = got_ref[:, n * width : (n + 1) * width].astype(jnp.float32)
        high, middle, low = (
            dot(jnp.where(turn == n, p, 0.0).astype(jnp.bfloat16), copies) for p in stress
        )
        force = force + ops * (high + middle + low)
    placer = jnp.transpose(member)[:BS].astype(jnp.bfloat16)
    return folded(dot(placer, stacked(folded(force, BS), 1)), BS)


def own_body(strains, field_ref, got_ref, out_ref):
    out_ref[...] = own_part(strains, field_ref[...], got_ref)


def own_of(field, got, strains):
    return pl.pallas_call(
        functools.partial(own_body, strains),
        compiler_params=LIMIT,
        cost_estimate=WORK,
        out_shape=jax.ShapeDtypeStruct(field.shape, jnp.float32),
    )(field, got)


def own_spread_body(strains, last_ref, got_ref, rest_ref, wide_hbm, cols_ref, *refs):
    down_ref, here_ref, up_ref, field_ref, returned_ref, wide_ref, arrival = refs
    steps = field_ref.shape[0] // PART
    part = PART * BS
    loads = [
        pltpu.make_async_copy(
            wide_hbm.at[pl.ds(n * part, part)], wide_ref.at[pl.ds(n * part, part)], arrival.at[n]
        )
        for n in range(steps)
    ]
    for load in loads:
        load.start()
    field_ref[...] = (rest_ref[...] + own_part(strains, last_ref[...], got_ref)) * SCALE
    for step, load in enumerate(loads):
        load.wait()
        spread_rows(PART, step, step, field_ref, wide_ref, returned_ref)
    spread_messages(field_ref, cols_ref, down_ref, here_ref, up_ref, returned_ref)


def own_spread_of(last, got, strains, rest, wide, cols_row):
    rows = last.shape[0]
    message = jax.ShapeDtypeStruct((rows, 2 * BS), jnp.float32)
    vector = jax.ShapeDtypeStruct(last.shape, jnp.float32)
    return pl.pallas_call(
        functools.partial(own_spread_body, strains),
        in_specs=[
            whole(last.shape),
            whole(got.shape),
            whole(rest.shape),
            pl.BlockSpec(memory_space=pl.ANY),
            whole(cols_row.shape),
        ],
        out_specs=[whole(v.shape) for v in (message, vector, message, vector)],
        compiler_params=LIMIT,
        cost_estimate=WORK,
        out_shape=[message, vector, message, vector],
        scratch_shapes=[
            pltpu.VMEM((rows, K * BS), jnp.float32),
            pltpu.VMEM(wide.shape, jnp.float32),
            pltpu.SemaphoreType.DMA((rows // PART,)),
        ],
    )(last, got, rest, pltpu.with_memory_space_constraint(wide, pltpu.HBM), cols_row)


def finish_body(ends_ref, got_ref, w0_ref, w1_ref, w2_ref, *refs):
    rest_ref, here_ref, lower_ref, upper_ref, solution_ref, residual_ref = refs
    total = jnp.sum(got_ref[...], axis=0, keepdims=True)
    moments = [total[:, n : n + 1] for n in range(2 * ITERS)]
    x_coef, r_coef = conjugate_coefficients(moments)
    lower, upper = arrived(ends_ref, lower_ref[:, BS:], upper_ref[:, BS:])
    w3 = (rest_ref[...] + here_ref[...] + (lower + upper)) * SCALE
    basis = [w0_ref[...], w1_ref[...], w2_ref[...], w3]
    solution_ref[...] = combine(x_coef, basis)
    residual_ref[...] = combine(r_coef, basis)


def ring(shard, axis, by):
    count = lax.axis_size(axis)
    return lax.ppermute(shard, axis, [(i, (i + by) % count) for i in range(count)])


def square(coefs):
    out = [0.0] * (2 * len(coefs) - 1)
    for i, a in enumerate(coefs):
        for j, b in enumerate(coefs):
            out[i + j] = out[i + j] + a * b
    return out


def plus(a, b):
    size = max(len(a), len(b))
    a, b = (list(v) + [0.0] * (size - len(v)) for v in (a, b))
    return [u + v for u, v in zip(a, b)]


def times(scalar, coefs):
    return [scalar * v for v in coefs]


def conjugate_coefficients(moments):
    x, r, p = [0.0], [1.0], [1.0]
    rr = moments[0]
    for step in range(ITERS):
        sq = square(p)
        bottom = sum(
            u * (moments[n + 1] * (1.0 / SCALE) + SHIFT * moments[n]) for n, u in enumerate(sq)
        )
        alpha = rr / bottom
        x = plus(x, times(alpha, p))
        image = plus([0.0] + times(1.0 / SCALE, p), times(SHIFT, p))
        r = plus(r, times(-alpha, image))
        if step < ITERS - 1:
            new = sum(u * moments[n] for n, u in enumerate(square(r)))
            p = plus(r, times(new / rr, p))
            rr = new
    return x, r


def combine(coefs, basis):
    total = coefs[0] * basis[0]
    for a, v in zip(coefs[1:], basis[1:]):
        total = total + a * v
    return total


def per_device(elem_ops, elem_stiff, owner, row_slot, couplings, coupling_cols, mass, rhs):
    rows_here = rhs.shape[0]
    owners = lax.axis_size("dev")
    count, strains, _ = elem_ops.shape
    capacity = 2 * count // owners
    slots = owners * capacity
    packed = pack(
        elem_ops.reshape(count, strains * BS), elem_stiff.T, owner.T, row_slot[None, :], slots, capacity
    )
    got = lax.all_to_all(
        packed, "dev", split_axis=0, concat_axis=0, tiled=True
    ).reshape(slots, -1)
    cols_row = coupling_cols.T.reshape(1, K * rows_here)
    wide = widened(couplings)
    place = lax.axis_index("group")
    ends = jnp.stack([place, lax.axis_size("group") - 1 - place]).astype(jnp.int32)

    def sent(down, here, up):
        return here, ring(up, "group", 1), ring(down, "group", -1)

    here, lower, upper = sent(*spread_of(rhs, wide, cols_row))
    rest = cross_of(ends, lower, rhs, upper, wide, coupling_cols, mass, here)
    *messages, w1 = own_spread_of(rhs, got, strains, rest, wide, cols_row)
    here, lower, upper = sent(*messages)
    own = own_of(w1, got, strains)
    w2 = cross_of(ends, lower, w1, upper, wide, coupling_cols, mass, here, own)
    lower, upper = ring(w2, "group", 1), ring(w2, "group", -1)
    own = own_of(w2, got, strains)
    members = lax.axis_size("group") * lax.axis_size("dev")
    rest, parts = cross_of(
        ends, lower, w2, upper, wide, coupling_cols, mass, own, earlier=(rhs, w1), members=members
    )
    got_parts = lax.all_to_all(parts, EVERY, 0, 0, tiled=True)
    here, lower, upper = sent(*spread_of(w2, wide, cols_row))
    operands = (ends, got_parts, rhs, w1, w2, rest, here, lower, upper)
    result = jax.ShapeDtypeStruct(rhs.shape, jnp.float32)
    return tuple(
        pl.pallas_call(
            finish_body,
            in_specs=[pl.BlockSpec(memory_space=pltpu.SMEM)]
            + [whole(v.shape) for v in operands[1:]],
            out_specs=[whole(rhs.shape)] * 2,
            compiler_params=LIMIT,
            out_shape=[result, result],
        )(*operands)
    )


def solution(mesh):
    placed = (
        P(EVERY, None, None),
        P(EVERY, None),
        P(EVERY, None),
        P(EVERY),
        P(EVERY, None, None, None),
        P(EVERY, None),
        P(EVERY, None),
        P(EVERY, None),
    )
    return jax.shard_map(
        per_device,
        mesh=mesh,
        in_specs=placed,
        out_specs=(P(EVERY, None), P(EVERY, None)),
        check_vma=False,
    )
```
